32 devices in a mesh: dp: 8 (over z, y), group: 4 (over x, core).
Axes of the slice: x: 2, y: 2, z: 4, core: 2. Of those that a mesh axis runs over, the one named last changes fastest.
Arguments:
- query_feats: bfloat16 [4096, 4096], P(('dp', 'group')), may hold values from -45 to 45
- passage_feats: bfloat16 [4096, 4096], P(('dp', 'group')), may hold values from -45 to 45
- head: bfloat16 [4096, 1024], replicated, may hold values from -0.09375 to 0.09375
- neg_ids: int32 [4096, 7], P(('dp', 'group')), may hold values from 0 to 4095, as said below
Outputs:
- head_grad: float32 [4096, 1024], P(('dp', 'group'))
- query_loss: float32 [4096], P(('dp', 'group'))
The draws below stay inside these ranges and needn't reach their ends.
Inputs may be any that keep to these rules, and one draw needn't show every extreme that they name: `neg_ids`: the 7 ids of a query name rows on 7 different devices, each with the query's group index and another dp index. Of the ids of one device's rows, at most 128 name rows of any one other device, and for every device some other device is named exactly 128 times.
All inputs are finite; a program needn't handle non-finite values.
Results may differ from the reference program's by a relative error of at most 0.0045.
The reference program's roundings to bfloat16 on the way count: a program that leaves them out, or rounds other values in their place, can miss the bound.
Values may be sent and summed in bfloat16 or wider, within the bound.
A program may use at most 128 MiB of HBM per device.

```python
import jax
import jax.numpy as jnp
from jax import lax

D = 4096
E = 1024
NEG = 7
TOK_DEV = 128
TOKENS = 4096
N_DP = 8
N_GROUP = 4


def feature_draw(key, salt):
    own_key = jax.random.fold_in(key, salt)
    key_noise, key_row, key_col = jax.random.split(own_key, 3)
    dev_total = N_DP * N_GROUP
    row_index = jnp.arange(TOKENS)
    device_pos = (row_index // TOK_DEV).astype(jnp.float32) / max(dev_total - 1, 1)
    rise = jnp.exp(jnp.log(3.0) * device_pos)[:, None]
    noise = jax.random.truncated_normal(key_noise, -4.0, 4.0, (TOKENS, D), jnp.float32)
    row_spread = jnp.exp(jax.random.uniform(key_row, (TOKENS, 1), jnp.float32, 0.0, jnp.log(10.0 / 3.0)))
    col_spread = jnp.exp(jax.random.uniform(key_col, (1, D), jnp.float32, 0.0, jnp.log(10.0)))
    return (noise * rise * row_spread * col_spread / 10.0).astype(jnp.bfloat16)


def draw_query_feats(key, part):
    return feature_draw(key, 11)


def draw_passage_feats(key, part):
    return feature_draw(key, 23)


def draw_neg_ids(key, part):
    dev_total = N_DP * N_GROUP
    other_count = N_DP - 1
    slot_total = NEG * TOK_DEV
    base_load = slot_total // other_count
    remainder = slot_total % other_count
    spread = max(0, min(base_load, TOK_DEV - base_load - 1))
    pair_count = (other_count - 2) // 2

    def one_device(device):
        dev_key = jax.random.fold_in(jax.random.fold_in(key, 37), device)
        key_pairs, key_amount, key_offset, key_local, key_order = jax.random.split(dev_key, 5)
        counts = base_load + (jnp.arange(other_count) < remainder).astype(jnp.int32)
        inner = jax.random.permutation(key_pairs, other_count - 2) + 1
        plus_side = inner[:pair_count]
        minus_side = inner[pair_count:2 * pair_count]
        amount = jax.random.randint(key_amount, (pair_count,), 0, spread + 1)
        counts = counts.at[plus_side].add(amount).at[minus_side].add(-amount)
        counts = counts.at[0].add(spread).at[other_count - 1].add(-spread)
        cumulative = jnp.cumsum(counts)
        slot_pos = jnp.arange(slot_total)
        owner_pos = jnp.sum((slot_pos[:, None] >= cumulative[None, :]).astype(jnp.int32), axis=1)
        offsets = 1 + jax.random.permutation(key_offset, other_count)[owner_pos]
        own_dp = device // N_GROUP
        own_group = device % N_GROUP
        owner_dp = (own_dp + offsets) % N_DP
        local_row = jax.random.randint(key_local, (slot_total,), 0, TOK_DEV)
        global_ids = (owner_dp * N_GROUP + own_group) * TOK_DEV + local_row
        table = global_ids.reshape(NEG, TOK_DEV).T
        order = jax.random.permutation(key_order, TOK_DEV)
        return table[order].astype(jnp.int32)
    return jax.vmap(one_device)(jnp.arange(dev_total)).reshape(TOKENS, NEG)


def bell_draw(rng, dims, scale, most, held_as=jnp.bfloat16):
    return jnp.clip(scale * jax.random.normal(rng, dims, jnp.float32), -most, most).astype(held_as)


def setup_inputs(seed: int = 0) -> dict:
    key_list = jax.random.split(jax.random.key(seed), 5)
    query_feats = draw_query_feats(jax.random.fold_in(key_list[4], 71), 0)
    passage_feats = draw_passage_feats(jax.random.fold_in(key_list[4], 71), 0)
    head = bell_draw(key_list[2], (D, E), D ** -0.5, 0.09375)
    neg_ids = draw_neg_ids(jax.random.fold_in(key_list[4], 71), 0)
    return dict(query_feats=query_feats, passage_feats=passage_feats, head=head, neg_ids=neg_ids)


scaling_divisor = 0.05
levels = 15.0
epsilon = 1e-06

def quantize(projected, low_bound, high_bound):
    as_float = projected.astype(jnp.float32)
    step_size = (high_bound - low_bound) / levels
    level_pos = (as_float - low_bound) / step_size
    quantized = low_bound + step_size * (level_pos - jnp.sin(2.0 * jnp.pi * level_pos) / (2.0 * jnp.pi))
    inverse = lax.rsqrt(lax.optimization_barrier(jnp.sum(quantized * quantized, axis=-1, keepdims=True)) + epsilon)
    return ((quantized * inverse).astype(jnp.bfloat16), quantized, inverse)

def norm_back(cotangent, quantized, inverse):
    inner_prod = lax.optimization_barrier(jnp.sum(quantized * cotangent, axis=-1, keepdims=True))
    return (inverse * cotangent - quantized * inverse ** 3 * inner_prod).astype(jnp.bfloat16)

def block_loss(anchor_vector_entries, inbatch_vector_entries, difficult_distractor_vectors, pos_mask):
    pairwise_cosine_scores = jnp.dot(anchor_vector_entries, inbatch_vector_entries.T, preferred_element_type=jnp.float32) / scaling_divisor
    difficult_distractor_scores = jnp.einsum('pgu,pu->pg', difficult_distractor_vectors.astype(jnp.float32), anchor_vector_entries.astype(jnp.float32)) / scaling_divisor
    positive = lax.optimization_barrier(jnp.sum(pairwise_cosine_scores * pos_mask, axis=1))
    exp_batch = jnp.exp(pairwise_cosine_scores)
    batch_total = lax.optimization_barrier(jnp.sum(exp_batch, axis=1))
    exp_pos = jnp.exp(positive)
    hard_exp = jnp.exp(difficult_distractor_scores)
    hard_total = exp_pos + lax.optimization_barrier(jnp.sum(hard_exp, axis=1))
    query_loss = jnp.log(batch_total) - positive + jnp.log(hard_total) - positive
    inbatch_normalized_share = (exp_batch / batch_total[:, None] - pos_mask * (2.0 - exp_pos / hard_total)[:, None]).astype(jnp.bfloat16)
    difficult_normalized_share = (hard_exp / hard_total[:, None]).astype(jnp.bfloat16)
    anchor_vector_derivative = (jnp.dot(inbatch_normalized_share, inbatch_vector_entries, preferred_element_type=jnp.float32) + jnp.einsum('mz,mzh->mh', difficult_normalized_share.astype(jnp.float32), difficult_distractor_vectors.astype(jnp.float32))) / scaling_divisor
    inbatch_vector_derivative = lax.dot_general(inbatch_normalized_share, anchor_vector_entries, (((0,), (0,)), ((), ())), preferred_element_type=jnp.float32) / scaling_divisor
    difficult_distractor_derivative = (difficult_normalized_share.astype(jnp.float32)[:, :, None] * anchor_vector_entries.astype(jnp.float32)[:, None, :] / scaling_divisor).astype(jnp.bfloat16)
    return (query_loss, anchor_vector_derivative, inbatch_vector_derivative, difficult_distractor_derivative)

def reference(query_feats, passage_feats, head, neg_ids):
    proj_query = jnp.dot(query_feats, head, preferred_element_type=jnp.float32).astype(jnp.bfloat16)
    proj_pass = jnp.dot(passage_feats, head, preferred_element_type=jnp.float32).astype(jnp.bfloat16)
    high_bound = jnp.maximum(lax.optimization_barrier(jnp.max(proj_query, axis=0)), lax.optimization_barrier(jnp.max(proj_pass, axis=0))).astype(jnp.float32)
    low_bound = jnp.minimum(lax.optimization_barrier(jnp.min(proj_query, axis=0)), lax.optimization_barrier(jnp.min(proj_pass, axis=0))).astype(jnp.float32)
    anchor_vector_entries, quant_query, inv_query = quantize(proj_query, low_bound, high_bound)
    pass_emb, quant_pass, inv_pass = quantize(proj_pass, low_bound, high_bound)
    difficult_distractor_vectors = pass_emb[neg_ids]
    cand_count = N_GROUP * TOK_DEV
    pos_mask = jnp.eye(cand_count, dtype=jnp.float32)
    query_blocks = anchor_vector_entries.reshape(N_DP, cand_count, E)
    pass_blocks = pass_emb.reshape(N_DP, cand_count, E)
    hard_blocks = difficult_distractor_vectors.reshape(N_DP, cand_count, NEG, E)

    def one_block(inputs):
        return block_loss(inputs[0], inputs[1], inputs[2], pos_mask)
    losses, query_grads, batch_grads, hard_grads = lax.map(one_block, (query_blocks, pass_blocks, hard_blocks))
    query_loss = losses.reshape(TOKENS)
    anchor_vector_derivative = query_grads.reshape(TOKENS, E)
    hard_flat = hard_grads.reshape(TOKENS * NEG, E).astype(jnp.float32)
    pass_grad = batch_grads.reshape(TOKENS, E) + jax.ops.segment_sum(hard_flat, neg_ids.reshape(-1).astype(jnp.int32), num_segments=TOKENS)
    proj_query_grad = norm_back(anchor_vector_derivative, quant_query, inv_query)
    proj_pass_grad = norm_back(pass_grad, quant_pass, inv_pass)
    head_grad = jnp.dot(query_feats.T, proj_query_grad, preferred_element_type=jnp.float32) + jnp.dot(passage_feats.T, proj_pass_grad, preferred_element_type=jnp.float32)
    return (head_grad, query_loss)
```

```python
import functools
import math

import jax
import jax.numpy as jnp
from jax import lax
from jax.experimental import pallas as pl
from jax.experimental.pallas import tpu as pltpu
from jax.sharding import PartitionSpec as P

scaling_divisor = 0.05
levels = 15.0
epsilon = 1e-06
MESH = pl.DeviceIdType.MESH
VMEM = pl.BlockSpec(memory_space=pltpu.VMEM)


def quantize(projected, low, stride, inv_stride):
    level = (projected.astype(jnp.float32) - low) * inv_stride
    turn = level - jnp.floor(level + 0.5)
    quarter = 0.25 - jnp.abs(jnp.abs(turn) - 0.25)
    angle = jnp.where(turn < 0, -quarter, quarter) * (2.0 * math.pi)
    square = angle * angle
    series = -1.0 / math.factorial(11)
    for order in (9, 7, 5, 3, 1):
        series = (-1.0) ** (order // 2) / math.factorial(order) + square * series
    return low + stride * (level - angle * series * (1.0 / (2.0 * math.pi)))


def norm_back(cotangent, quantized, inverse):
    inner_prod = jnp.sum(quantized * cotangent, axis=-1, keepdims=True)
    return (inverse * cotangent - quantized * (inverse**3 * inner_prod)).astype(jnp.bfloat16)


def dot_nn(a, b):
    return jnp.dot(a, b, preferred_element_type=jnp.float32)


def dot_nt(a, b):
    return lax.dot_general(a, b, (((1,), (1,)), ((), ())), preferred_element_type=jnp.float32)


def dot_tn(a, b):
    return lax.dot_general(a, b, (((0,), (0,)), ((), ())), preferred_element_type=jnp.float32)


def remote(src, dst, send, recv, device):
    return pltpu.make_async_remote_copy(
        src_ref=src,
        dst_ref=dst,
        send_sem=send,
        recv_sem=recv,
        device_id=device,
        device_id_type=MESH,
    )


def step_kernel(
    n_dp, n_group, inner, chunks,
    proj_query, proj_pass, stats, query_feats, pass_feats, named, out, loss,
    stats_group, stats_dp, stats_mid,
    emb_query, emb_pass, quant_query, quant_pass, inv_query, inv_pass,
    batch_query, batch_pass, dp_query, dp_pass, hard_exp,
    batch_out, batch_in, hard_out, hard_in,
    feats, turned, dy, gathered, total, pair_out, pair_in, line_out, line_in, kept,
    s_stat_g, r_stat_g, s_stat_d, r_stat_d, s_feat, r_feat,
    s_line, s_pair, r_dp, s_batch, r_batch, s_bw, r_bw, s_hw, r_hw,
    s_dy, r_dy, s_p, r_p, s_l, r_l, *staged
):
    me_d, me_g = lax.axis_index("dp"), lax.axis_index("group")
    line = n_dp // inner
    z, y = me_d // inner, lax.rem(me_d, inner)
    rows, emb = proj_query.shape
    wide = emb // chunks
    block = out.shape[0]
    columns = lambda c: pl.ds(c * wide, wide)
    group_at = lambda k: lax.rem(me_g + k, n_group)
    group_from = lambda k: lax.rem(me_g + n_group - k, n_group)
    dp_at = lambda k: lax.rem(me_d + k, n_dp)
    dp_from = lambda k: lax.rem(me_d + n_dp - k, n_dp)

    cut_feats = (staged[0].at[0], staged[0].at[1]) if staged else (query_feats, pass_feats)

    def feat_copy(i, k):
        src = cut_feats[i]
        return remote(
            src.at[group_at(k)], feats.at[i, k], s_feat.at[i, k], r_feat.at[i, k], (me_d, group_at(k))
        )

    def largest(src, landing, send, recv, count, target):
        copies = []
        for k in range(1, count):
            copies.append(remote(src, landing.at[k], send.at[k], recv.at[k], target(k)))
            copies[-1].start()
        value = src[...]
        for k in range(1, count):
            copies[k - 1].wait()
            value = jnp.maximum(value, landing[k])
        return value

    if staged:
        for i, whole in enumerate((query_feats, pass_feats)):
            for d in range(n_dp):
                for g in range(n_group):
                    staged[0][i, g, :, d * block : (d + 1) * block] = whole[
                        :, (d * n_group + g) * block : (d * n_group + g + 1) * block
                    ]

    stats_mid[...] = largest(
        stats, stats_group, s_stat_g, r_stat_g, n_group, lambda k: (me_d, group_at(k))
    )
    for i in range(2):
        for k in range(1, n_group):
            feat_copy(i, k).start()
    bounds = largest(stats_mid, stats_dp, s_stat_d, r_stat_d, n_dp, lambda k: (dp_at(k), me_g))
    high, low = bounds[0:1], -bounds[1:2]
    stride = (high - low) / levels
    inv_stride = 1.0 / stride

    items = ((emb_pass, batch_pass, dp_pass), (emb_query, batch_query, dp_query))

    def slot_copy(i, source, src, send, target):
        return remote(src, items[i][2].at[source], send, r_dp.at[i, source], (target, me_g))

    def forwards(i, at, src, rightward, leftward):
        source = at * inner + y
        copies = []
        if rightward:
            copies.append((z < line - 1, slot_copy(i, source, src, s_line.at[i, 0, at], dp_at(inner))))
        if leftward:
            copies.append((z > 0, slot_copy(i, source, src, s_line.at[i, 1, at], dp_from(inner))))
        for k in range(1, inner):
            target = z * inner + lax.rem(y + k, inner)
            copies.append((None, slot_copy(i, source, src, s_pair.at[i, k, at], target)))
        return copies

    def each(copies, act):
        for condition, copy in copies:
            if condition is None:
                act(copy)
            else:
                pl.when(condition)(functools.partial(act, copy))

    def start(copy):
        copy.start()

    def wait_send(copy):
        copy.wait_send()

    def batch_copy(i, k):
        return remote(
            items[i][0], items[i][1].at[k], s_batch.at[i, k], r_batch.at[i, k], (me_d, group_at(k))
        )

    def start_own(i):
        each(forwards(i, z, items[i][0], True, True), start)
        for k in range(1, n_group):
            batch_copy(i, k).start()

    def relay(i, s):
        for at, inside, onward in ((z - s, z >= s, True), (z + s, z + s < line, False)):

            @pl.when(inside)
            def _(at=at, onward=onward):
                source = at * inner + y
                arrived = items[i][2].at[source]
                slot_copy(i, source, arrived, s_line.at[i, 0, at], me_d).wait_recv()
                each(forwards(i, at, arrived, onward, not onward), start)

    def wait_pairs(i):
        for k in range(1, inner):
            for at in range(line):
                source = at * inner + lax.rem(y + k, inner)
                arrived = items[i][2].at[source]
                slot_copy(i, source, arrived, s_pair.at[i, k, at], me_d).wait_recv()

    def wait_all_sent(i):
        each(forwards(i, z, items[i][0], True, True), wait_send)
        for s in range(1, line):
            for at, inside, onward in ((z - s, z >= s, True), (z + s, z + s < line, False)):

                @pl.when(inside)
                def _(at=at, onward=onward):
                    arrived = items[i][2].at[at * inner + y]
                    each(forwards(i, at, arrived, onward, not onward), wait_send)

    def embed(projected, quant, inverse, emb_ref):
        value = quantize(projected[...], low, stride, inv_stride)
        inv = lax.rsqrt(jnp.sum(value * value, axis=-1, keepdims=True) + epsilon)
        quant[...] = value
        inverse[...] = inv
        emb_ref[...] = (value * inv).astype(jnp.bfloat16)

    embed(proj_pass, quant_pass, inv_pass, emb_pass)
    start_own(0)
    embed(proj_query, quant_query, inv_query, emb_query)
    for s in range(1, line):
        relay(0, s)
    start_own(1)

    for i in range(2):
        for k in range(1, n_group):
            feat_copy(i, k).wait()
        lanes = pl.ds(i * rows, rows)
        turned[0, :, lanes] = cut_feats[i][me_g].T
        for k in range(1, n_group):
            turned[k, :, lanes] = feats[i, k].T

    for k in range(1, n_group):
        batch_copy(0, k).wait()
    wait_pairs(0)
    if line > 1:
        relay(1, 1)

    def over_dp(step, value):
        if n_dp > 16:
            return lax.fori_loop(1, n_dp, step, value)
        for k in range(1, n_dp):
            value = step(k, value)
        return value

    query = emb_query[...]
    eye = (
        lax.broadcasted_iota(jnp.int32, (rows, rows), 0)
        == lax.broadcasted_iota(jnp.int32, (rows, rows), 1)
    ).astype(jnp.float32)
    place = lax.broadcasted_iota(jnp.int32, (rows, rows), 1)
    batch_block = lambda k: emb_pass[...] if k == 0 else batch_pass[k]
    scores = [dot_nt(query, batch_block(k)) / scaling_divisor for k in range(n_group)]
    positive = jnp.sum(scores[0] * eye, axis=1, keepdims=True)
    exp_batch = [jnp.exp(score) for score in scores]
    batch_total = sum(jnp.sum(value, axis=1, keepdims=True) for value in exp_batch)
    exp_pos = jnp.exp(positive)

    def hard_step(k, hard_sum):
        source = dp_at(k)
        score = dot_nt(query, dp_pass[source]) / scaling_divisor
        here = named[:, 0:1] == place + source * rows
        for n in range(1, named.shape[1]):
            here = here | (named[:, n : n + 1] == place + source * rows)
        value = jnp.where(here, jnp.exp(score), 0.0)
        hard_exp[k] = value
        return hard_sum + value

    hard_sum = over_dp(hard_step, jnp.zeros((rows, rows), jnp.float32))
    hard_total = exp_pos + jnp.sum(hard_sum, axis=1, keepdims=True)
    column = jnp.log(batch_total) - positive + jnp.log(hard_total) - positive
    loss[...] = jnp.sum(column * eye, axis=0, keepdims=True)

    def weight_copy(k):
        return remote(
            batch_out.at[k], batch_in.at[k], s_bw.at[k], r_bw.at[k], (me_d, group_from(k))
        )

    def hard_copy(k):
        return remote(hard_out.at[k], hard_in.at[k], s_hw.at[k], r_hw.at[k], (dp_at(k), me_g))

    for k in range(n_group):
        weight = exp_batch[k] / batch_total
        if k == 0:
            weight = weight - eye * (2.0 - exp_pos / hard_total)
        batch_out[k] = weight.astype(jnp.bfloat16)
        if k:
            weight_copy(k).start()

    def hard_send(k, nothing):
        hard_out[k] = (hard_exp[k] / hard_total).astype(jnp.bfloat16)
        hard_copy(k).start()
        return nothing

    over_dp(hard_send, 0)
    if line > 2:
        relay(1, 2)

    grad = dot_nn(batch_out[0], emb_pass[...])
    for k in range(1, n_group):
        grad += dot_nn(batch_out[k], batch_pass[k])
    grad = over_dp(lambda k, value: value + dot_nn(hard_out[k], dp_pass[dp_at(k)]), grad)
    dy[0] = norm_back(grad / scaling_divisor, quant_query[...], inv_query[...])

    def dy_copy(i, c, k):
        return remote(
            dy.at[i, :, columns(c)], gathered.at[k, pl.ds(i * rows, rows), columns(c)],
            s_dy.at[i, c, k], r_dy.at[i, c, k], (me_d, group_at(k)),
        )

    for c in range(chunks):
        for k in range(1, n_group):
            dy_copy(0, c, k).start()
    for s in range(3, line):
        relay(1, s)

    for k in range(1, n_group):
        batch_copy(1, k).wait()
        weight_copy(k).wait()
    grad = dot_tn(batch_out[0], emb_query[...])
    for k in range(1, n_group):
        grad += dot_tn(batch_in[k], batch_query[n_group - k])
    grad = grad / scaling_divisor
    wait_pairs(1)

    def hard_back(k, value):
        hard_copy(k).wait()
        weight = hard_in[k]
        one = jnp.sum(weight.astype(jnp.float32), axis=1, keepdims=True)
        hard = (one * dp_query[dp_from(k)].astype(jnp.float32) * (1.0 / scaling_divisor)).astype(
            jnp.bfloat16
        )
        chosen = jnp.where(weight.astype(jnp.float32) != 0, 1.0, 0.0).astype(jnp.bfloat16)
        return value + dot_tn(chosen, hard)

    dy[1] = norm_back(over_dp(hard_back, grad), quant_pass[...], inv_pass[...])
    for c in range(chunks):
        for k in range(1, n_group):
            dy_copy(1, c, k).start()

    def pair_copy(c, k):
        target = z * inner + lax.rem(y + k, inner)
        return remote(
            pair_out.at[c, k - 1], pair_in.at[c, k - 1], s_p.at[c, k], r_p.at[c, k], (target, me_g)
        )

    def line_copy(c, j):
        target = lax.rem(z + j, line) * inner + y
        return remote(
            line_out.at[c, j], line_in.at[c, j], s_l.at[c, j], r_l.at[c, j], (target, me_g)
        )

    def first(c):
        part = dot_nn(turned[0, :, 0:rows], dy[0, :, columns(c)])
        part += dot_nn(turned[0, :, rows:], dy[1, :, columns(c)])
        for k in range(1, n_group):
            dy_copy(0, c, k).wait()
            dy_copy(1, c, k).wait()
            part += dot_nn(turned[k], gathered[k, :, columns(c)])
        total[c] = part.reshape(n_dp, block, wide)
        for k in range(1, inner):
            for at in range(line):
                pair_out[c, k - 1, at] = total[c, at * inner + lax.rem(y + k, inner)].astype(
                    jnp.bfloat16
                )
            pair_copy(c, k).start()

    def second(c):
        for k in range(1, inner):
            pair_copy(c, k).wait()

        def summed(at):
            value = total[c, at * inner + y]
            for k in range(1, inner):
                value += pair_in[c, k - 1, at].astype(jnp.float32)
            return value

        for j in range(1, line):
            line_out[c, j] = summed(lax.rem(z + j, line)).astype(jnp.bfloat16)
            line_copy(c, j).start()
        kept[c] = summed(z)

    def third(c):
        value = kept[c]
        for j in range(1, line):
            line_copy(c, j).wait()
            value += line_in[c, j].astype(jnp.float32)
        out[:, columns(c)] = value

    for c in range(chunks):
        first(c)
        if c:
            second(c - 1)
    second(chunks - 1)
    for i in range(2):
        wait_all_sent(i)
    for c in range(chunks):
        third(c)


def whole_step(proj_query, proj_pass, stats, query_feats, pass_feats, named, n_dp, n_group, block):
    inner = 2 if n_dp % 2 == 0 else 1
    line = n_dp // inner
    rows, emb = proj_query.shape
    depth = n_dp * block
    inside = query_feats.ndim == 2
    chunks = max(1, emb // 256)
    wide = emb // chunks
    bf16 = lambda *shape: pltpu.VMEM(shape, jnp.bfloat16)
    f32 = lambda *shape: pltpu.VMEM(shape, jnp.float32)
    sems = lambda *shape: [pltpu.SemaphoreType.DMA(shape)]
    pairs = lambda *shape: sems(*shape) * 2
    return pl.pallas_call(
        functools.partial(step_kernel, n_dp, n_group, inner, chunks),
        out_shape=(
            jax.ShapeDtypeStruct((block, emb), jnp.float32),
            jax.ShapeDtypeStruct((1, rows), jnp.float32),
        ),
        in_specs=[VMEM] * 6,
        out_specs=(VMEM, VMEM),
        scratch_shapes=[
            f32(n_group, 2, emb), f32(n_dp, 2, emb), f32(2, emb),
            bf16(rows, emb), bf16(rows, emb), f32(rows, emb), f32(rows, emb), f32(rows, 1), f32(rows, 1),
            bf16(n_group, rows, emb), bf16(n_group, rows, emb), bf16(n_dp, rows, emb), bf16(n_dp, rows, emb),
            f32(n_dp, rows, rows),
            bf16(n_group, rows, rows), bf16(n_group, rows, rows), bf16(n_dp, rows, rows), bf16(n_dp, rows, rows),
            bf16(2, n_group, rows, depth), bf16(n_group, depth, 2 * rows), bf16(2, rows, emb),
            bf16(n_group, 2 * rows, emb),
            f32(chunks, n_dp, block, wide),
            bf16(chunks, max(1, inner - 1), line, block, wide),
            bf16(chunks, max(1, inner - 1), line, block, wide),
            bf16(chunks, line, block, wide), bf16(chunks, line, block, wide),
            f32(chunks, block, wide),
        ]
        + pairs(n_group) + pairs(n_dp) + pairs(2, n_group)
        + sems(2, 2, line) + sems(2, inner, line) + sems(2, n_dp) + pairs(2, n_group)
        + pairs(n_group) + pairs(n_dp)
        + pairs(2, chunks, n_group) + pairs(chunks, inner) + pairs(chunks, line)
        + ([bf16(2, n_group, rows, depth)] if inside else []),
        compiler_params=pltpu.CompilerParams(has_side_effects=True, vmem_limit_bytes=67043328),
        name="step",
    )(proj_query, proj_pass, stats, query_feats, pass_feats, named)


def chip_kernel(
    n_dp, n_group, chunks, slabs,
    pass_hbm, query_hbm, head_hbm, ids,
    out, loss,
    lhs, head, proj, stats, stats_dp, stats_mid, stats_group, ids_own, ids_in,
    quant, inv, batch, dp_pass, dp_query, emb_dp,
    exp_batch, hard_exp, batch_out, batch_in, row_out, row_in,
    sent_feats, turned, dy, total, pair_out, pair_in, line_out, line_in, kept,
    l_feat, l_head, l_own, s_stat_d, r_stat_d, s_stat_g, r_stat_g, s_ids, r_ids,
    s_line, s_pair, r_dp, s_batch, r_batch, s_feat, r_feat, s_bw, r_bw, s_row, r_row,
    s_dyq, r_dyq, s_dyp, r_dyp, s_p, r_p, s_l, r_l,
):
    me_d, me_g = lax.axis_index("dp"), lax.axis_index("group")
    inner = 2
    line = n_dp // inner
    z, y = me_d // inner, lax.rem(me_d, inner)
    chips = n_group // 2
    chip, core = me_g // 2, lax.rem(me_g, 2)
    rows, emb = proj.shape[1:]
    wide = emb // chunks
    slab = head.shape[0] // slabs
    block = out.shape[0]
    columns = lambda c: pl.ds(c * wide, wide)
    own_rows = lambda g: pl.ds(pl.multiple_of(g * rows, rows), rows)
    group_at = lambda k: lax.rem(me_g + k, n_group)
    dp_at = lambda k: lax.rem(me_d + k, n_dp)
    z_at = lambda k: lax.rem(z + k, line)
    partner = chip * 2 + 1 - core
    beside = [lax.rem(chip + j, chips) * 2 + core for j in range(1, chips)]
    relayed = [lax.rem(chip + j, chips) * 2 + 1 - core for j in range(1, chips)]
    others = [partner] + beside + relayed
    across = z * inner + 1 - y

    unsent = []

    def send(src, dst, send_sem, recv_sem, device, condition=None):
        copy = remote(src, dst, send_sem, recv_sem, device)
        if condition is None:
            copy.start()
        else:
            pl.when(condition)(copy.start)
        unsent.append((condition, copy))

    def arrived(dst, recv_sem):
        remote(dst, dst, recv_sem, recv_sem, (me_d, partner)).wait_recv()

    barrier = pltpu.get_barrier_semaphore()
    peers = [(me_d, group_at(k)) for k in range(1, n_group)] + [(dp_at(k), me_g) for k in range(1, n_dp)]
    for peer in peers:
        pl.semaphore_signal(barrier, inc=1, device_id=peer, device_id_type=MESH)

    loads = []
    for i, source in enumerate((pass_hbm, query_hbm)):
        loads.append(pltpu.make_async_copy(source, lhs.at[pl.ds(i * rows, rows)], l_feat.at[i]))
    for s in range(slabs):
        piece = pl.ds(s * slab, slab)
        loads.append(pltpu.make_async_copy(head_hbm.at[piece], head.at[piece], l_head.at[s]))
    for copy in loads:
        copy.start()
    ids_own[...] = jnp.full(ids_own.shape, -1, jnp.int32)
    ids_own[0 : ids.shape[0]] = ids[...]
    loads[0].wait()
    loads[1].wait()
    value = None
    for s in range(slabs):
        loads[2 + s].wait()
        part = dot_nn(lhs[:, s * slab : (s + 1) * slab], head[s * slab : (s + 1) * slab])
        value = part if value is None else value + part
    rounded = value.astype(jnp.bfloat16)
    proj[0] = rounded[:rows]
    proj[1] = rounded[rows:]
    seen = rounded.astype(jnp.float32)
    stats[0:1] = jnp.max(seen, axis=0, keepdims=True)
    stats[1:2] = -jnp.min(seen, axis=0, keepdims=True)
    pl.semaphore_wait(barrier, len(peers))

    for k in range(1, n_dp):
        send(stats, stats_dp.at[k], s_stat_d.at[k], r_stat_d.at[k], (dp_at(k), me_g))

    dp_bufs = (dp_pass, dp_query)

    def along(i, at, src, rightward, leftward):
        source = at * inner + y
        dst = dp_bufs[i].at[source]
        if rightward:
            send(src, dst, s_line.at[i, 0, at], r_dp.at[i, source], (dp_at(inner), me_g), z < line - 1)
        if leftward:
            send(src, dst, s_line.at[i, 1, at], r_dp.at[i, source], (lax.rem(me_d + n_dp - inner, n_dp), me_g), z > 0)

    def over(i, at, src):
        source = at * inner + y
        send(src, dp_bufs[i].at[source], s_pair.at[i, at], r_dp.at[i, source], (across, me_g))

    relay_log = []

    def relay(i, s):
        for at, inside, onward in ((z - s, z >= s, 0), (z + s, z + s < line, 1)):
            source = at * inner + y
            block_ref = dp_bufs[i].at[source]
            if onward == 0:
                target, more = dp_at(inner), inside & (z < line - 1)
            else:
                target, more = lax.rem(me_d + n_dp - inner, n_dp), inside & (z > 0)
            forward = remote(
                block_ref, block_ref, s_line.at[i, onward, at], r_dp.at[i, source], (target, me_g)
            )
            side = remote(block_ref, block_ref, s_pair.at[i, at], r_dp.at[i, source], (across, me_g))

            @pl.when(inside)
            def _(block_ref=block_ref, source=source, side=side):
                arrived(block_ref, r_dp.at[i, source])

            pl.when(more)(forward.start)
            pl.when(inside)(side.start)
            unsent.append((more, forward))
            unsent.append((inside, side))

    along(0, z, proj.at[0], True, True)
    over(0, z, proj.at[0])
    for k in range(1, n_dp):
        send(ids_own, ids_in.at[k], s_ids.at[k], r_ids.at[k], (dp_at(k), me_g))

    bounds = stats[...]
    for k in range(1, n_dp):
        arrived(stats_dp.at[k], r_stat_d.at[k])
        bounds = jnp.maximum(bounds, stats_dp[k])
    stats_mid[...] = bounds
    for k in range(1, n_group):
        send(stats_mid, stats_group.at[k], s_stat_g.at[k], r_stat_g.at[k], (me_d, group_at(k)))
    for k in range(1, n_group):
        arrived(stats_group.at[k], r_stat_g.at[k])
        bounds = jnp.maximum(bounds, stats_group[k])
    high, low = bounds[0:1], -bounds[1:2]
    stride = (high - low) / levels
    inv_stride = 1.0 / stride

    def embed(projected):
        value = quantize(projected, low, stride, inv_stride)
        inverse = lax.rsqrt(jnp.sum(value * value, axis=-1, keepdims=True) + epsilon)
        return value, inverse, (value * inverse).astype(jnp.bfloat16)

    for i in range(2):
        quant[i], inv[i], batch[i, me_g] = embed(proj[i])
        own = batch.at[i, me_g]
        for m, target in enumerate([partner] + beside):
            send(own, own, s_batch.at[i, m], r_batch.at[i, me_g], (me_d, target))

    def hand_over(i):
        for m, source in enumerate(beside):
            landed = batch.at[i, source]
            arrived(landed, r_batch.at[i, source])
            send(landed, landed, s_batch.at[i, chips + m], r_batch.at[i, source], (me_d, partner))

    relay(0, 1)
    hand_over(0)

    for i in (1, 0):
        for d in range(n_dp * n_group):
            sent_feats[i, d // n_group, d % n_group] = lhs[
                i * rows : (i + 1) * rows, d * block : (d + 1) * block
            ].T
        for m, target in enumerate(others):
            send(
                sent_feats.at[i, :, target], turned.at[i, :, :, own_rows(me_g)],
                s_feat.at[i, m], r_feat.at[i, me_g], (me_d, target),
            )
    stay = [
        pltpu.make_async_copy(
            sent_feats.at[i, :, me_g], turned.at[i, :, :, own_rows(me_g)], l_own.at[i]
        )
        for i in range(2)
    ]
    for copy in stay:
        copy.start()

    query = batch[1, me_g]
    eye = (
        lax.broadcasted_iota(jnp.int32, (rows, rows), 0)
        == lax.broadcasted_iota(jnp.int32, (rows, rows), 1)
    ).astype(jnp.float32)
    place = lax.broadcasted_iota(jnp.int32, (rows, rows), 0)

    def named(rows_of, device):
        base = (device * n_group + me_g) * rows
        here = rows_of[0:1] == place + base
        for n in range(1, ids.shape[0]):
            here = here | (rows_of[n : n + 1] == place + base)
        return here

    def hard_scores(source):
        _, _, block_emb = embed(dp_pass[source])
        emb_dp[source] = block_emb
        score = dot_nt(block_emb, query) / scaling_divisor
        hard_exp[source] = jnp.where(named(ids_own[...], source), jnp.exp(score), 0.0)

    relay(0, 2) if line > 2 else None
    along(1, z, batch.at[1, me_g], True, True)
    arrived(dp_pass.at[across], r_dp.at[0, across])
    hard_scores(across)
    hand_over(1)
    for s in range(3, line):
        relay(0, s)
    over(1, z, batch.at[1, me_g])

    for source in [partner] + relayed:
        arrived(batch.at[0, source], r_batch.at[0, source])
    own_score = dot_nt(batch[0, me_g], query) / scaling_divisor
    positive = jnp.sum(own_score * eye, axis=0, keepdims=True)
    own_exp = jnp.exp(own_score)
    batch_total = jnp.sum(own_exp, axis=0, keepdims=True)
    for m, source in enumerate(others):
        weight = jnp.exp(dot_nt(batch[0, source], query) / scaling_divisor)
        exp_batch[m] = weight
        batch_total += jnp.sum(weight, axis=0, keepdims=True)
    exp_pos = jnp.exp(positive)

    for k in range(1, line):
        hard_scores(z_at(k) * inner + y)
        if k == 1:
            relay(1, 1)
    for k in range(1, line):
        source = z_at(k) * inner + 1 - y
        arrived(dp_pass.at[source], r_dp.at[0, source])
        hard_scores(source)

    hard_sum = hard_exp[dp_at(1)]
    for k in range(2, n_dp):
        hard_sum += hard_exp[dp_at(k)]
    hard_total = exp_pos + jnp.sum(hard_sum, axis=0, keepdims=True)
    loss[...] = jnp.log(batch_total) - positive + jnp.log(hard_total) - positive

    for m, target in enumerate(others):
        batch_out[target] = (exp_batch[m] / batch_total).astype(jnp.bfloat16)
        send(batch_out.at[target], batch_in.at[me_g], s_bw.at[m], r_bw.at[me_g], (me_d, target))
    own_weight = (own_exp / batch_total - eye * (2.0 - exp_pos / hard_total)).astype(jnp.bfloat16)
    grad = dot_tn(own_weight, batch[0, me_g])
    for source in others:
        grad += dot_tn(batch_out[source], batch[0, source])
    for k in range(1, n_dp):
        source = dp_at(k)
        weight = (hard_exp[source] / hard_total).astype(jnp.bfloat16)
        row = jnp.sum(weight.astype(jnp.float32), axis=0, keepdims=True)
        row_out[k] = jnp.broadcast_to(row, row_out.shape[1:])
        send(row_out.at[k], row_in.at[k], s_row.at[k], r_row.at[k], (source, me_g))
        grad += dot_tn(weight, emb_dp[source])
    if line > 2:
        relay(1, 2)
    dy[1, own_rows(me_g)] = norm_back(grad / scaling_divisor, quant[1], inv[1])
    own = dy.at[1, own_rows(me_g)]
    for m, target in enumerate([partner] + beside):
        send(own, own, s_dyq.at[m], r_dyq.at[me_g], (me_d, target))

    for source in [partner] + relayed:
        arrived(batch.at[1, source], r_batch.at[1, source])
    grad = dot_nn(own_weight, query)
    for source in others:
        arrived(batch_in.at[source], r_bw.at[source])
        grad += dot_nn(batch_in[source], batch[1, source])
    grad = grad / scaling_divisor

    for m, source in enumerate(beside):
        landed = dy.at[1, own_rows(source)]
        arrived(landed, r_dyq.at[source])
        send(landed, landed, s_dyq.at[chips + m], r_dyq.at[source], (me_d, partner))
    for k in range(1, n_dp):
        arrived(ids_in.at[k], r_ids.at[k])
        arrived(row_in.at[k], r_row.at[k])

    def hard_back(source, k):
        weight = jnp.sum(row_in[k][0:1] * eye, axis=1, keepdims=True)
        hard = (weight * dp_query[source].astype(jnp.float32) * (1.0 / scaling_divisor)).astype(
            jnp.bfloat16
        )
        chosen = jnp.where(named(ids_in[k], me_d), 1.0, 0.0).astype(jnp.bfloat16)
        return dot_nn(chosen, hard)

    def behind(source):
        return lax.rem(me_d + n_dp - source, n_dp)

    arrived(dp_query.at[across], r_dp.at[1, across])
    grad += hard_back(across, behind(across))

    for copy in stay:
        copy.wait()
    for source in others:
        arrived(turned.at[1, :, :, own_rows(source)], r_feat.at[1, source])
    for source in [partner] + relayed:
        arrived(dy.at[1, own_rows(source)], r_dyq.at[source])
    depth = n_dp * block
    seen_rows = lambda i: turned[i].reshape(depth, n_group * rows)
    for c in range(chunks):
        total[c] = dot_nn(seen_rows(1), dy[1, :, columns(c)]).reshape(n_dp, block, wide)
        if c == 1:
            for s in range(3, line):
                relay(1, s)
    for source in others:
        arrived(turned.at[0, :, :, own_rows(source)], r_feat.at[0, source])
    for k in range(1, line):
        source = z_at(k) * inner + y
        grad += hard_back(source, behind(source))
    for k in range(1, line):
        source = z_at(k) * inner + 1 - y
        arrived(dp_query.at[source], r_dp.at[1, source])
        grad += hard_back(source, behind(source))

    dy[0, own_rows(me_g)] = norm_back(grad, quant[0], inv[0])
    for c in range(chunks):
        own = dy.at[0, own_rows(me_g), columns(c)]
        for m, target in enumerate(beside):
            send(own, own, s_dyp.at[c, 1 + m], r_dyp.at[c, me_g], (me_d, target))
        send(own, own, s_dyp.at[c, 0], r_dyp.at[c, me_g], (me_d, partner))

    def pass_on(c):
        for m, source in enumerate(beside):
            landed = dy.at[0, own_rows(source), columns(c)]
            arrived(landed, r_dyp.at[c, source])
            send(landed, landed, s_dyp.at[c, chips + m], r_dyp.at[c, source], (me_d, partner))

    def first(c):
        for source in [partner] + relayed:
            arrived(dy.at[0, own_rows(source), columns(c)], r_dyp.at[c, source])
        part = dot_nn(seen_rows(0), dy[0, :, columns(c)]).reshape(n_dp, block, wide)
        total[c] += part
        for at in range(line):
            pair_out[c, at] = total[c, at * inner + 1 - y].astype(jnp.bfloat16)
        send(pair_out.at[c], pair_in.at[c], s_p.at[c], r_p.at[c], (across, me_g))

    def second(c):
        arrived(pair_in.at[c], r_p.at[c])
        summed = lambda at: total[c, at * inner + y] + pair_in[c, at].astype(jnp.float32)
        for j in range(1, line):
            line_out[c, j] = summed(z_at(j)).astype(jnp.bfloat16)
            send(
                line_out.at[c, j], line_in.at[c, j], s_l.at[c, j], r_l.at[c, j],
                (z_at(j) * inner + y, me_g),
            )
        kept[c] = summed(z)

    def third(c):
        value = kept[c]
        for j in range(1, line):
            arrived(line_in.at[c, j], r_l.at[c, j])
            value += line_in[c, j].astype(jnp.float32)
        out[:, columns(c)] = value

    lag = 3
    pass_on(0)
    for c in range(chunks):
        if c + 1 < chunks:
            pass_on(c + 1)
        first(c)
        if c >= lag:
            second(c - lag)
    for c in range(max(0, chunks - lag), chunks):
        second(c)
    for c in range(chunks):
        third(c)
    for condition, copy in unsent:
        if condition is None:
            copy.wait_send()
        else:
            pl.when(condition)(copy.wait_send)


def chip_step(pass_feats, query_feats, head, ids, n_dp, n_group, block):
    rows, width = pass_feats.shape
    emb = head.shape[1]
    line, chips = n_dp // 2, n_group // 2
    chunks = emb // 128
    slabs = max(1, width // 512)
    wide = emb // chunks
    bf16 = lambda *shape: pltpu.VMEM(shape, jnp.bfloat16)
    f32 = lambda *shape: pltpu.VMEM(shape, jnp.float32)
    i32 = lambda *shape: pltpu.VMEM(shape, jnp.int32)
    sems = lambda *shape: [pltpu.SemaphoreType.DMA(shape)]
    pairs = lambda *shape: sems(*shape) * 2
    anywhere = pl.BlockSpec(memory_space=pl.ANY)
    return pl.pallas_call(
        functools.partial(chip_kernel, n_dp, n_group, chunks, slabs),
        out_shape=(
            jax.ShapeDtypeStruct((block, emb), jnp.float32),
            jax.ShapeDtypeStruct((1, rows), jnp.float32),
        ),
        in_specs=[anywhere, anywhere, anywhere, VMEM],
        out_specs=(VMEM, VMEM),
        scratch_shapes=[
            bf16(2 * rows, width), bf16(width, emb), bf16(2, rows, emb),
            f32(2, emb), f32(n_dp, 2, emb), f32(2, emb), f32(n_group, 2, emb),
            i32(8, rows), i32(n_dp, 8, rows),
            f32(2, rows, emb), f32(2, rows, 1), bf16(2, n_group, rows, emb),
            bf16(n_dp, rows, emb), bf16(n_dp, rows, emb), bf16(n_dp, rows, emb),
            f32(n_group, rows, rows), f32(n_dp, rows, rows),
            bf16(n_group, rows, rows), bf16(n_group, rows, rows),
            f32(n_dp, 8, rows), f32(n_dp, 8, rows),
            bf16(2, n_dp, n_group, block, rows), bf16(2, n_dp, block, n_group * rows),
            bf16(2, n_group * rows, emb),
            f32(chunks, n_dp, block, wide),
            bf16(chunks, line, block, wide), bf16(chunks, line, block, wide),
            bf16(chunks, line, block, wide), bf16(chunks, line, block, wide),
            f32(chunks, block, wide),
        ]
        + sems(2) + sems(slabs) + sems(2) + pairs(n_dp) + pairs(n_group) + pairs(n_dp)
        + sems(2, 2, line) + sems(2, line) + sems(2, n_dp)
        + sems(2, 2 * chips) + sems(2, n_group)
        + sems(2, n_group) + sems(2, n_group)
        + pairs(n_group) + pairs(n_dp)
        + sems(2 * chips) + sems(n_group)
        + sems(chunks, 2 * chips) + sems(chunks, n_group)
        + pairs(chunks) + pairs(chunks, line),
        compiler_params=pltpu.CompilerParams(
            has_side_effects=True, collective_id=0, vmem_limit_bytes=60 * 2**20
        ),
        name="chip_step",
    )(pass_feats, query_feats, head, ids)


def body(query_feats, passage_feats, head, neg_ids):
    rows, width = query_feats.shape
    emb = head.shape[1]
    n_dp = lax.axis_size("dp")
    n_group = lax.axis_size("group")
    block = width // (n_dp * n_group)
    if n_dp <= 16 and n_dp % 2 == 0 and n_group % 2 == 0 and block % 128 == 0:
        head_grad, query_loss = chip_step(
            passage_feats, query_feats, head, neg_ids.T, n_dp, n_group, block
        )
        return (head_grad, query_loss.reshape(rows))

    def cut(feats):
        if block % 128 == 0:
            return feats
        feats = feats.reshape(rows, n_dp, n_group, block)
        return feats.transpose(2, 0, 1, 3).reshape(n_group, rows, n_dp * block)

    proj_query = jnp.dot(query_feats, head, preferred_element_type=jnp.float32).astype(jnp.bfloat16)
    proj_pass = jnp.dot(passage_feats, head, preferred_element_type=jnp.float32).astype(
        jnp.bfloat16
    )
    col_high = jnp.maximum(jnp.max(proj_query, axis=0), jnp.max(proj_pass, axis=0)).astype(
        jnp.float32
    )
    col_low = jnp.minimum(jnp.min(proj_query, axis=0), jnp.min(proj_pass, axis=0)).astype(
        jnp.float32
    )
    named = (neg_ids // (n_group * rows)) * rows + neg_ids % rows
    head_grad, query_loss = whole_step(
        proj_query, proj_pass, jnp.stack([col_high, -col_low]), cut(query_feats),
        cut(passage_feats), named, n_dp, n_group, block,
    )
    return (head_grad, query_loss.reshape(rows))


def solution(mesh):
    return jax.shard_map(
        body,
        mesh=mesh,
        in_specs=(
            P(("dp", "group"), None),
            P(("dp", "group"), None),
            P(),
            P(("dp", "group"), None),
        ),
        out_specs=(P(("dp", "group"), None), P(("dp", "group"))),
        check_vma=False,
    )
```

```python
import functools
import math

import jax
import jax.numpy as jnp
from jax import lax
from jax.experimental import pallas as pl
from jax.experimental.pallas import tpu as pltpu
from jax.sharding import PartitionSpec as P

scaling_divisor = 0.05
levels = 15.0
epsilon = 1e-06
MESH = pl.DeviceIdType.MESH
VMEM = pl.BlockSpec(memory_space=pltpu.VMEM)


def quantize(projected, low, stride, inv_stride):
    level = (projected.astype(jnp.float32) - low) * inv_stride
    turn = level - jnp.floor(level + 0.5)
    quarter = 0.25 - jnp.abs(jnp.abs(turn) - 0.25)
    angle = jnp.where(turn < 0, -quarter, quarter) * (2.0 * math.pi)
    square = angle * angle
    series = -1.0 / math.factorial(11)
    for order in (9, 7, 5, 3, 1):
        series = (-1.0) ** (order // 2) / math.factorial(order) + square * series
    return low + stride * (level - angle * series * (1.0 / (2.0 * math.pi)))


def norm_back(cotangent, quantized, inverse):
    inner_prod = jnp.sum(quantized * cotangent, axis=-1, keepdims=True)
    return (inverse * cotangent - quantized * (inverse**3 * inner_prod)).astype(jnp.bfloat16)


def dot_nn(a, b):
    return jnp.dot(a, b, preferred_element_type=jnp.float32)


def dot_nt(a, b):
    return lax.dot_general(a, b, (((1,), (1,)), ((), ())), preferred_element_type=jnp.float32)


def dot_tn(a, b):
    return lax.dot_general(a, b, (((0,), (0,)), ((), ())), preferred_element_type=jnp.float32)


def remote(src, dst, send, recv, device):
    return pltpu.make_async_remote_copy(
        src_ref=src,
        dst_ref=dst,
        send_sem=send,
        recv_sem=recv,
        device_id=device,
        device_id_type=MESH,
    )


def step_kernel(
    n_dp, n_group, inner, chunks,
    proj_query, proj_pass, stats, query_feats, pass_feats, named, out, loss,
    stats_group, stats_dp, stats_mid,
    emb_query, emb_pass, quant_query, quant_pass, inv_query, inv_pass,
    batch_query, batch_pass, dp_query, dp_pass, hard_exp,
    batch_out, batch_in, hard_out, hard_in,
    feats, turned, dy, gathered, total, pair_out, pair_in, line_out, line_in, kept,
    s_stat_g, r_stat_g, s_stat_d, r_stat_d, s_feat, r_feat,
    s_line, s_pair, r_dp, s_batch, r_batch, s_bw, r_bw, s_hw, r_hw,
    s_dy, r_dy, s_p, r_p, s_l, r_l, *staged
):
    me_d, me_g = lax.axis_index("dp"), lax.axis_index("group")
    line = n_dp // inner
    z, y = me_d // inner, lax.rem(me_d, inner)
    rows, emb = proj_query.shape
    wide = emb // chunks
    block = out.shape[0]
    columns = lambda c: pl.ds(c * wide, wide)
    group_at = lambda k: lax.rem(me_g + k, n_group)
    group_from = lambda k: lax.rem(me_g + n_group - k, n_group)
    dp_at = lambda k: lax.rem(me_d + k, n_dp)
    dp_from = lambda k: lax.rem(me_d + n_dp - k, n_dp)

    cut_feats = (staged[0].at[0], staged[0].at[1]) if staged else (query_feats, pass_feats)

    def feat_copy(i, k):
        src = cut_feats[i]
        return remote(
            src.at[group_at(k)], feats.at[i, k], s_feat.at[i, k], r_feat.at[i, k], (me_d, group_at(k))
        )

    def largest(src, landing, send, recv, count, target):
        copies = []
        for k in range(1, count):
            copies.append(remote(src, landing.at[k], send.at[k], recv.at[k], target(k)))
            copies[-1].start()
        value = src[...]
        for k in range(1, count):
            copies[k - 1].wait()
            value = jnp.maximum(value, landing[k])
        return value

    if staged:
        for i, whole in enumerate((query_feats, pass_feats)):
            for d in range(n_dp):
                for g in range(n_group):
                    staged[0][i, g, :, d * block : (d + 1) * block] = whole[
                        :, (d * n_group + g) * block : (d * n_group + g + 1) * block
                    ]

    stats_mid[...] = largest(
        stats, stats_group, s_stat_g, r_stat_g, n_group, lambda k: (me_d, group_at(k))
    )
    for i in range(2):
        for k in range(1, n_group):
            feat_copy(i, k).start()
    bounds = largest(stats_mid, stats_dp, s_stat_d, r_stat_d, n_dp, lambda k: (dp_at(k), me_g))
    high, low = bounds[0:1], -bounds[1:2]
    stride = (high - low) / levels
    inv_stride = 1.0 / stride

    items = ((emb_pass, batch_pass, dp_pass), (emb_query, batch_query, dp_query))

    def slot_copy(i, source, src, send, target):
        return remote(src, items[i][2].at[source], send, r_dp.at[i, source], (target, me_g))

    def forwards(i, at, src, rightward, leftward):
        source = at * inner + y
        copies = []
        if rightward:
            copies.append((z < line - 1, slot_copy(i, source, src, s_line.at[i, 0, at], dp_at(inner))))
        if leftward:
            copies.append((z > 0, slot_copy(i, source, src, s_line.at[i, 1, at], dp_from(inner))))
        for k in range(1, inner):
            target = z * inner + lax.rem(y + k, inner)
            copies.append((None, slot_copy(i, source, src, s_pair.at[i, k, at], target)))
        return copies

    def each(copies, act):
        for condition, copy in copies:
            if condition is None:
                act(copy)
            else:
                pl.when(condition)(functools.partial(act, copy))

    def start(copy):
        copy.start()

    def wait_send(copy):
        copy.wait_send()

    def batch_copy(i, k):
        return remote(
            items[i][0], items[i][1].at[k], s_batch.at[i, k], r_batch.at[i, k], (me_d, group_at(k))
        )

    def start_own(i):
        each(forwards(i, z, items[i][0], True, True), start)
        for k in range(1, n_group):
            batch_copy(i, k).start()

    def relay(i, s):
        for at, inside, onward in ((z - s, z >= s, True), (z + s, z + s < line, False)):

            @pl.when(inside)
            def _(at=at, onward=onward):
                source = at * inner + y
                arrived = items[i][2].at[source]
                slot_copy(i, source, arrived, s_line.at[i, 0, at], me_d).wait_recv()
                each(forwards(i, at, arrived, onward, not onward), start)

    def wait_pairs(i):
        for k in range(1, inner):
            for at in range(line):
                source = at * inner + lax.rem(y + k, inner)
                arrived = items[i][2].at[source]
                slot_copy(i, source, arrived, s_pair.at[i, k, at], me_d).wait_recv()

    def wait_all_sent(i):
        each(forwards(i, z, items[i][0], True, True), wait_send)
        for s in range(1, line):
            for at, inside, onward in ((z - s, z >= s, True), (z + s, z + s < line, False)):

                @pl.when(inside)
                def _(at=at, onward=onward):
                    arrived = items[i][2].at[at * inner + y]
                    each(forwards(i, at, arrived, onward, not onward), wait_send)

    def embed(projected, quant, inverse, emb_ref):
        value = quantize(projected[...], low, stride, inv_stride)
        inv = lax.rsqrt(jnp.sum(value * value, axis=-1, keepdims=True) + epsilon)
        quant[...] = value
        inverse[...] = inv
        emb_ref[...] = (value * inv).astype(jnp.bfloat16)

    embed(proj_pass, quant_pass, inv_pass, emb_pass)
    start_own(0)
    embed(proj_query, quant_query, inv_query, emb_query)
    for s in range(1, line):
        relay(0, s)
    start_own(1)

    for i in range(2):
        for k in range(1, n_group):
            feat_copy(i, k).wait()
        lanes = pl.ds(i * rows, rows)
        turned[0, :, lanes] = cut_feats[i][me_g].T
        for k in range(1, n_group):
            turned[k, :, lanes] = feats[i, k].T

    for k in range(1, n_group):
        batch_copy(0, k).wait()
    wait_pairs(0)
    if line > 1:
        relay(1, 1)

    def over_dp(step, value):
        if n_dp > 16:
            return lax.fori_loop(1, n_dp, step, value)
        for k in range(1, n_dp):
            value = step(k, value)
        return value

    query = emb_query[...]
    eye = (
        lax.broadcasted_iota(jnp.int32, (rows, rows), 0)
        == lax.broadcasted_iota(jnp.int32, (rows, rows), 1)
    ).astype(jnp.float32)
    place = lax.broadcasted_iota(jnp.int32, (rows, rows), 1)
    batch_block = lambda k: emb_pass[...] if k == 0 else batch_pass[k]
    scores = [dot_nt(query, batch_block(k)) / scaling_divisor for k in range(n_group)]
    positive = jnp.sum(scores[0] * eye, axis=1, keepdims=True)
    exp_batch = [jnp.exp(score) for score in scores]
    batch_total = sum(jnp.sum(value, axis=1, keepdims=True) for value in exp_batch)
    exp_pos = jnp.exp(positive)

    def hard_step(k, hard_sum):
        source = dp_at(k)
        score = dot_nt(query, dp_pass[source]) / scaling_divisor
        here = named[:, 0:1] == place + source * rows
        for n in range(1, named.shape[1]):
            here = here | (named[:, n : n + 1] == place + source * rows)
        value = jnp.where(here, jnp.exp(score), 0.0)
        hard_exp[k] = value
        return hard_sum + value

    hard_sum = over_dp(hard_step, jnp.zeros((rows, rows), jnp.float32))
    hard_total = exp_pos + jnp.sum(hard_sum, axis=1, keepdims=True)
    column = jnp.log(batch_total) - positive + jnp.log(hard_total) - positive
    loss[...] = jnp.sum(column * eye, axis=0, keepdims=True)

    def weight_copy(k):
        return remote(
            batch_out.at[k], batch_in.at[k], s_bw.at[k], r_bw.at[k], (me_d, group_from(k))
        )

    def hard_copy(k):
        return remote(hard_out.at[k], hard_in.at[k], s_hw.at[k], r_hw.at[k], (dp_at(k), me_g))

    for k in range(n_group):
        weight = exp_batch[k] / batch_total
        if k == 0:
            weight = weight - eye * (2.0 - exp_pos / hard_total)
        batch_out[k] = weight.astype(jnp.bfloat16)
        if k:
            weight_copy(k).start()

    def hard_send(k, nothing):
        hard_out[k] = (hard_exp[k] / hard_total).astype(jnp.bfloat16)
        hard_copy(k).start()
        return nothing

    over_dp(hard_send, 0)
    if line > 2:
        relay(1, 2)

    grad = dot_nn(batch_out[0], emb_pass[...])
    for k in range(1, n_group):
        grad += dot_nn(batch_out[k], batch_pass[k])
    grad = over_dp(lambda k, value: value + dot_nn(hard_out[k], dp_pass[dp_at(k)]), grad)
    dy[0] = norm_back(grad / scaling_divisor, quant_query[...], inv_query[...])

    def dy_copy(i, c, k):
        return remote(
            dy.at[i, :, columns(c)], gathered.at[k, pl.ds(i * rows, rows), columns(c)],
            s_dy.at[i, c, k], r_dy.at[i, c, k], (me_d, group_at(k)),
        )

    for c in range(chunks):
        for k in range(1, n_group):
            dy_copy(0, c, k).start()
    for s in range(3, line):
        relay(1, s)

    for k in range(1, n_group):
        batch_copy(1, k).wait()
        weight_copy(k).wait()
    grad = dot_tn(batch_out[0], emb_query[...])
    for k in range(1, n_group):
        grad += dot_tn(batch_in[k], batch_query[n_group - k])
    grad = grad / scaling_divisor
    wait_pairs(1)

    def hard_back(k, value):
        hard_copy(k).wait()
        weight = hard_in[k]
        one = jnp.sum(weight.astype(jnp.float32), axis=1, keepdims=True)
        hard = (one * dp_query[dp_from(k)].astype(jnp.float32) * (1.0 / scaling_divisor)).astype(
            jnp.bfloat16
        )
        chosen = jnp.where(weight.astype(jnp.float32) != 0, 1.0, 0.0).astype(jnp.bfloat16)
        return value + dot_tn(chosen, hard)

    dy[1] = norm_back(over_dp(hard_back, grad), quant_pass[...], inv_pass[...])
    for c in range(chunks):
        for k in range(1, n_group):
            dy_copy(1, c, k).start()

    def pair_copy(c, k):
        target = z * inner + lax.rem(y + k, inner)
        return remote(
            pair_out.at[c, k - 1], pair_in.at[c, k - 1], s_p.at[c, k], r_p.at[c, k], (target, me_g)
        )

    def line_copy(c, j):
        target = lax.rem(z + j, line) * inner + y
        return remote(
            line_out.at[c, j], line_in.at[c, j], s_l.at[c, j], r_l.at[c, j], (target, me_g)
        )

    def first(c):
        part = dot_nn(turned[0, :, 0:rows], dy[0, :, columns(c)])
        part += dot_nn(turned[0, :, rows:], dy[1, :, columns(c)])
        for k in range(1, n_group):
            dy_copy(0, c, k).wait()
            dy_copy(1, c, k).wait()
            part += dot_nn(turned[k], gathered[k, :, columns(c)])
        total[c] = part.reshape(n_dp, block, wide)
        for k in range(1, inner):
            for at in range(line):
                pair_out[c, k - 1, at] = total[c, at * inner + lax.rem(y + k, inner)].astype(
                    jnp.bfloat16
                )
            pair_copy(c, k).start()

    def second(c):
        for k in range(1, inner):
            pair_copy(c, k).wait()

        def summed(at):
            value = total[c, at * inner + y]
            for k in range(1, inner):
                value += pair_in[c, k - 1, at].astype(jnp.float32)
            return value

        for j in range(1, line):
            line_out[c, j] = summed(lax.rem(z + j, line)).astype(jnp.bfloat16)
            line_copy(c, j).start()
        kept[c] = summed(z)

    def third(c):
        value = kept[c]
        for j in range(1, line):
            line_copy(c, j).wait()
            value += line_in[c, j].astype(jnp.float32)
        out[:, columns(c)] = value

    for c in range(chunks):
        first(c)
        if c:
            second(c - 1)
    second(chunks - 1)
    for i in range(2):
        wait_all_sent(i)
    for c in range(chunks):
        third(c)


def whole_step(proj_query, proj_pass, stats, query_feats, pass_feats, named, n_dp, n_group, block):
    inner = 2 if n_dp % 2 == 0 else 1
    line = n_dp // inner
    rows, emb = proj_query.shape
    depth = n_dp * block
    inside = query_feats.ndim == 2
    chunks = max(1, emb // 256)
    wide = emb // chunks
    bf16 = lambda *shape: pltpu.VMEM(shape, jnp.bfloat16)
    f32 = lambda *shape: pltpu.VMEM(shape, jnp.float32)
    sems = lambda *shape: [pltpu.SemaphoreType.DMA(shape)]
    pairs = lambda *shape: sems(*shape) * 2
    return pl.pallas_call(
        functools.partial(step_kernel, n_dp, n_group, inner, chunks),
        out_shape=(
            jax.ShapeDtypeStruct((block, emb), jnp.float32),
            jax.ShapeDtypeStruct((1, rows), jnp.float32),
        ),
        in_specs=[VMEM] * 6,
        out_specs=(VMEM, VMEM),
        scratch_shapes=[
            f32(n_group, 2, emb), f32(n_dp, 2, emb), f32(2, emb),
            bf16(rows, emb), bf16(rows, emb), f32(rows, emb), f32(rows, emb), f32(rows, 1), f32(rows, 1),
            bf16(n_group, rows, emb), bf16(n_group, rows, emb), bf16(n_dp, rows, emb), bf16(n_dp, rows, emb),
            f32(n_dp, rows, rows),
            bf16(n_group, rows, rows), bf16(n_group, rows, rows), bf16(n_dp, rows, rows), bf16(n_dp, rows, rows),
            bf16(2, n_group, rows, depth), bf16(n_group, depth, 2 * rows), bf16(2, rows, emb),
            bf16(n_group, 2 * rows, emb),
            f32(chunks, n_dp, block, wide),
            bf16(chunks, max(1, inner - 1), line, block, wide),
            bf16(chunks, max(1, inner - 1), line, block, wide),
            bf16(chunks, line, block, wide), bf16(chunks, line, block, wide),
            f32(chunks, block, wide),
        ]
        + pairs(n_group) + pairs(n_dp) + pairs(2, n_group)
        + sems(2, 2, line) + sems(2, inner, line) + sems(2, n_dp) + pairs(2, n_group)
        + pairs(n_group) + pairs(n_dp)
        + pairs(2, chunks, n_group) + pairs(chunks, inner) + pairs(chunks, line)
        + ([bf16(2, n_group, rows, depth)] if inside else []),
        compiler_params=pltpu.CompilerParams(has_side_effects=True, vmem_limit_bytes=67043328),
        name="step",
    )(proj_query, proj_pass, stats, query_feats, pass_feats, named)


def chip_kernel(
    n_dp, n_group, chunks, slabs,
    pass_hbm, query_hbm, head_hbm, ids,
    out, loss,
    lhs, head, proj, stats, stats_dp, stats_mid, stats_group, ids_own, ids_in,
    quant, inv, batch, dp_pass, dp_query, emb_dp,
    exp_batch, hard_exp, batch_out, batch_in, row_out, row_in,
    sent_feats, turned, dy, total, pair_out, pair_in, line_out, line_in, kept,
    l_feat, l_head, l_own, s_stat_d, r_stat_d, s_stat_g, r_stat_g, s_ids, r_ids,
    s_line, s_pair, r_dp, s_half, r_half, s_batch, r_batch, s_feat, r_feat, s_bw, r_bw, s_row, r_row,
    s_dyq, r_dyq, s_dyp, r_dyp, s_p, r_p, s_l, r_l,
):
    me_d, me_g = lax.axis_index("dp"), lax.axis_index("group")
    inner = 2
    line = n_dp // inner
    z, y = me_d // inner, lax.rem(me_d, inner)
    chips = n_group // 2
    chip, core = me_g // 2, lax.rem(me_g, 2)
    rows, emb = proj.shape[1:]
    wide = emb // chunks
    slab = emb // slabs
    block = out.shape[0]
    columns = lambda c: pl.ds(c * wide, wide)
    own_rows = lambda g: pl.ds(pl.multiple_of(g * rows, rows), rows)
    group_at = lambda k: lax.rem(me_g + k, n_group)
    dp_at = lambda k: lax.rem(me_d + k, n_dp)
    dp_from = lambda k: lax.rem(me_d + n_dp - k, n_dp)
    z_at = lambda k: lax.rem(z + k, line)

    def plane(k):
        value = z
        for bit in range(k.bit_length()):
            if k >> bit & 1:
                value = value + (1 - 2 * lax.rem(z // (1 << bit), 2)) * (1 << bit)
        return value

    half = rows // 2
    partner = chip * 2 + 1 - core
    beside = [lax.rem(chip + j, chips) * 2 + core for j in range(1, chips)]
    relayed = [lax.rem(chip + j, chips) * 2 + 1 - core for j in range(1, chips)]
    others = [partner] + beside + relayed
    across = z * inner + 1 - y

    unsent = []

    def send(src, dst, send_sem, recv_sem, device, condition=None):
        copy = remote(src, dst, send_sem, recv_sem, device)
        if condition is None:
            copy.start()
        else:
            pl.when(condition)(copy.start)
        unsent.append((condition, copy))

    def arrived(dst, recv_sem):
        remote(dst, dst, recv_sem, recv_sem, (me_d, partner)).wait_recv()

    barrier = pltpu.get_barrier_semaphore()
    peers = [(me_d, group_at(k)) for k in range(1, n_group)] + [(dp_at(k), me_g) for k in range(1, n_dp)]
    for peer in peers:
        pl.semaphore_signal(barrier, inc=1, device_id=peer, device_id_type=MESH)

    loads = []
    for i, source in enumerate((pass_hbm, query_hbm)):
        loads.append(pltpu.make_async_copy(source, lhs.at[pl.ds(i * rows, rows)], l_feat.at[i]))
    for s in range(slabs):
        piece = pl.ds(s * slab, slab)
        loads.append(
            pltpu.make_async_copy(head_hbm.at[:, piece], head.at[:, piece], l_head.at[s])
        )
    for copy in loads:
        copy.start()
    ids_own[...] = jnp.full(ids_own.shape, -1, jnp.int32)
    ids_own[0 : ids.shape[0]] = ids[...]
    loads[0].wait()
    loads[1].wait()
    for s in range(slabs):
        loads[2 + s].wait()
        piece = slice(s * slab, (s + 1) * slab)
        rounded = dot_nn(lhs[...], head[:, piece]).astype(jnp.bfloat16)
        proj[0, :, piece] = rounded[:rows]
        proj[1, :, piece] = rounded[rows:]
        seen = rounded.astype(jnp.float32)
        stats[0:1, piece] = jnp.max(seen, axis=0, keepdims=True)
        stats[1:2, piece] = -jnp.min(seen, axis=0, keepdims=True)
    pl.semaphore_wait(barrier, len(peers))

    for k in range(1, n_dp):
        send(stats, stats_dp.at[k], s_stat_d.at[k], r_stat_d.at[k], (dp_at(k), me_g))

    dp_bufs = (dp_pass, dp_query)

    def along(i, at, src, rightward, leftward):
        source = at * inner + y
        dst = dp_bufs[i].at[source]
        if rightward:
            send(src, dst, s_line.at[i, 0, at], r_dp.at[i, source], (dp_at(inner), me_g), z < line - 1)
        if leftward:
            send(src, dst, s_line.at[i, 1, at], r_dp.at[i, source], (dp_from(inner), me_g), z > 0)

    def over(i, at, src):
        source = at * inner + y
        send(src, dp_bufs[i].at[source], s_pair.at[i, at], r_dp.at[i, source], (across, me_g))

    def relay(i, s):
        for at, inside, onward in ((z - s, z >= s, 0), (z + s, z + s < line, 1)):
            source = at * inner + y
            landed = dp_bufs[i].at[source]
            part = landed.at[pl.ds(0, half)]
            if onward == 0:
                target, more, twin = dp_at(inner), inside & (z < line - 1), lax.rem(z, 2) == 1
            else:
                target, more, twin = dp_from(inner), inside & (z > 0), lax.rem(z, 2) == 0
            recv = r_dp.at[i, source]
            steps = [(more, remote(landed, landed, s_line.at[i, onward, at], recv, (target, me_g)))]
            side = remote(landed, landed, s_pair.at[i, at], recv, (across, me_g))
            if s == 1:
                steps.append((inside & jnp.logical_not(twin), side))
                steps.append(
                    (inside & twin, remote(part, part, s_pair.at[i, at], recv, (across, me_g)))
                )
            else:
                steps.append((inside, side))

            @pl.when(inside)
            def _(landed=landed, recv=recv):
                arrived(landed, recv)

            for condition, copy in steps:
                pl.when(condition)(copy.start)
                unsent.append((condition, copy))

    def lower(i):
        arrived(dp_bufs[i].at[across], r_dp.at[i, across])
        part = dp_bufs[i].at[across, pl.ds(half, half)]
        send(part, part, s_half.at[i], r_half.at[i], (plane(1) * inner + y, me_g))

    def gathered(i, k):
        source = plane(k) * inner + 1 - y
        landed = dp_bufs[i].at[source]
        if k == 1:
            arrived(landed.at[pl.ds(0, half)], r_dp.at[i, source])
            arrived(landed.at[pl.ds(half, half)], r_half.at[i])
        else:
            arrived(landed, r_dp.at[i, source])
        return source

    def turn(i):
        for d in range(n_dp * n_group):
            sent_feats[i, d // n_group, d % n_group] = lhs[
                i * rows : (i + 1) * rows, d * block : (d + 1) * block
            ].T

    def send_feats(i, which):
        for m, target in enumerate(others):
            if m in which:
                send(
                    sent_feats.at[i, :, target], turned.at[i, :, :, own_rows(me_g)],
                    s_feat.at[i, m], r_feat.at[i, me_g], (me_d, target),
                )

    along(0, z, proj.at[0], True, True)
    over(0, z, proj.at[0])
    for k in range(1, n_dp):
        send(ids_own, ids_in.at[k], s_ids.at[k], r_ids.at[k], (dp_at(k), me_g))

    turn(1)
    bounds = stats[...]
    for k in range(1, n_dp):
        arrived(stats_dp.at[k], r_stat_d.at[k])
        bounds = jnp.maximum(bounds, stats_dp[k])
    stats_mid[...] = bounds
    for k in range(1, n_group):
        send(stats_mid, stats_group.at[k], s_stat_g.at[k], r_stat_g.at[k], (me_d, group_at(k)))
    send_feats(1, range(chips))
    relay(0, 1)
    lower(0)
    for k in range(1, n_group):
        arrived(stats_group.at[k], r_stat_g.at[k])
        bounds = jnp.maximum(bounds, stats_group[k])
    high, low = bounds[0:1], -bounds[1:2]
    stride = (high - low) / levels
    inv_stride = 1.0 / stride

    def embed(projected):
        value = quantize(projected, low, stride, inv_stride)
        inverse = lax.rsqrt(jnp.sum(value * value, axis=-1, keepdims=True) + epsilon)
        return value, inverse, (value * inverse).astype(jnp.bfloat16)

    for i in range(2):
        quant[i], inv[i], batch[i, me_g] = embed(proj[i])
        own = batch.at[i, me_g]
        for m, target in enumerate([partner] + beside):
            send(own, own, s_batch.at[i, m], r_batch.at[i, me_g], (me_d, target))

    def hand_over(i):
        for m, source in enumerate(beside):
            landed = batch.at[i, source]
            arrived(landed, r_batch.at[i, source])
            send(landed, landed, s_batch.at[i, chips + m], r_batch.at[i, source], (me_d, partner))

    send_feats(1, range(chips, n_group))
    turn(0)
    stay = [
        pltpu.make_async_copy(
            sent_feats.at[i, :, me_g], turned.at[i, :, :, own_rows(me_g)], l_own.at[i]
        )
        for i in range(2)
    ]
    for copy in stay:
        copy.start()

    query = batch[1, me_g]
    eye = (
        lax.broadcasted_iota(jnp.int32, (rows, rows), 0)
        == lax.broadcasted_iota(jnp.int32, (rows, rows), 1)
    ).astype(jnp.float32)
    place = lax.broadcasted_iota(jnp.int32, (rows, rows), 0)

    def named(rows_of, device):
        base = (device * n_group + me_g) * rows
        here = rows_of[0:1] == place + base
        for n in range(1, ids.shape[0]):
            here = here | (rows_of[n : n + 1] == place + base)
        return here

    def hard_scores(source):
        _, _, block_emb = embed(dp_pass[source])
        emb_dp[source] = block_emb
        score = dot_nt(block_emb, query) / scaling_divisor
        hard_exp[source] = jnp.where(named(ids_own[...], source), jnp.exp(score), 0.0)

    hard_scores(across)
    if line > 2:
        relay(0, 2)
    along(1, z, batch.at[1, me_g], True, True)
    hand_over(0)
    send_feats(0, range(chips))
    for s in range(3, line):
        relay(0, s)
    over(1, z, batch.at[1, me_g])
    hand_over(1)

    for source in [partner] + relayed:
        arrived(batch.at[0, source], r_batch.at[0, source])
    own_score = dot_nt(batch[0, me_g], query) / scaling_divisor
    positive = jnp.sum(own_score * eye, axis=0, keepdims=True)
    own_exp = jnp.exp(own_score)
    batch_total = jnp.sum(own_exp, axis=0, keepdims=True)
    for m, source in enumerate(others):
        weight = jnp.exp(dot_nt(batch[0, source], query) / scaling_divisor)
        exp_batch[m] = weight
        batch_total += jnp.sum(weight, axis=0, keepdims=True)
    exp_pos = jnp.exp(positive)

    for k in range(1, line):
        hard_scores(plane(k) * inner + y)
    relay(1, 1)
    lower(1)
    for k in range(1, line):
        hard_scores(gathered(0, k))

    hard_sum = hard_exp[dp_at(1)]
    for k in range(2, n_dp):
        hard_sum += hard_exp[dp_at(k)]
    hard_total = exp_pos + jnp.sum(hard_sum, axis=0, keepdims=True)
    loss[...] = jnp.log(batch_total) - positive + jnp.log(hard_total) - positive

    for m, target in enumerate(others):
        batch_out[target] = (exp_batch[m] / batch_total).astype(jnp.bfloat16)
        send(batch_out.at[target], batch_in.at[me_g], s_bw.at[m], r_bw.at[me_g], (me_d, target))
    own_weight = (own_exp / batch_total - eye * (2.0 - exp_pos / hard_total)).astype(jnp.bfloat16)
    grad = dot_tn(own_weight, batch[0, me_g])
    for source in others:
        grad += dot_tn(batch_out[source], batch[0, source])
    for k in range(1, n_dp):
        source = dp_at(k)
        weight = (hard_exp[source] / hard_total).astype(jnp.bfloat16)
        row = jnp.sum(weight.astype(jnp.float32), axis=0, keepdims=True)
        row_out[k] = jnp.broadcast_to(row, row_out.shape[1:])
        send(row_out.at[k], row_in.at[k], s_row.at[k], r_row.at[k], (source, me_g))
        grad += dot_tn(weight, emb_dp[source])
    dy[1, own_rows(me_g)] = norm_back(grad / scaling_divisor, quant[1], inv[1])
    own = dy.at[1, own_rows(me_g)]
    for m, target in enumerate([partner] + beside):
        send(own, own, s_dyq.at[m], r_dyq.at[me_g], (me_d, target))
    send_feats(0, range(chips, n_group))
    if line > 2:
        relay(1, 2)

    for source in [partner] + relayed:
        arrived(batch.at[1, source], r_batch.at[1, source])
    grad = dot_nn(own_weight, query)
    for source in others:
        arrived(batch_in.at[source], r_bw.at[source])
        grad += dot_nn(batch_in[source], batch[1, source])
    grad = grad / scaling_divisor
    for k in range(1, n_dp):
        arrived(ids_in.at[k], r_ids.at[k])

    def hard_back(source):
        k = lax.rem(me_d + n_dp - source, n_dp)
        arrived(row_in.at[k], r_row.at[k])
        weight = jnp.sum(row_in[k][0:1] * eye, axis=1, keepdims=True)
        hard = (weight * dp_query[source].astype(jnp.float32) * (1.0 / scaling_divisor)).astype(
            jnp.bfloat16
        )
        chosen = jnp.where(named(ids_in[k], me_d), 1.0, 0.0).astype(jnp.bfloat16)
        return dot_nn(chosen, hard)

    grad += hard_back(across)
    for s in range(3, line):
        relay(1, s)
    for m, source in enumerate(beside):
        landed = dy.at[1, own_rows(source)]
        arrived(landed, r_dyq.at[source])
        send(landed, landed, s_dyq.at[chips + m], r_dyq.at[source], (me_d, partner))
    for k in range(1, line):
        grad += hard_back(plane(k) * inner + y)
    for copy in stay:
        copy.wait()
    for source in others:
        arrived(turned.at[1, :, :, own_rows(source)], r_feat.at[1, source])
    for source in [partner] + relayed:
        arrived(dy.at[1, own_rows(source)], r_dyq.at[source])
    depth = n_dp * block
    seen_rows = lambda i: turned[i].reshape(depth, n_group * rows)
    from_query = lambda c: dot_nn(seen_rows(1), dy[1, :, columns(c)]).reshape(n_dp, block, wide)
    early = min(2, chunks)
    for c in range(early):
        total[c] = from_query(c)
    for k in range(1, line):
        grad += hard_back(gathered(1, k))

    dy[0, own_rows(me_g)] = norm_back(grad, quant[0], inv[0])
    for c in range(chunks):
        own = dy.at[0, own_rows(me_g), columns(c)]
        for m, target in enumerate(beside):
            send(own, own, s_dyp.at[c, 1 + m], r_dyp.at[c, me_g], (me_d, target))
        send(own, own, s_dyp.at[c, 0], r_dyp.at[c, me_g], (me_d, partner))

    def pass_on(c):
        for m, source in enumerate(beside):
            landed = dy.at[0, own_rows(source), columns(c)]
            arrived(landed, r_dyp.at[c, source])
            send(landed, landed, s_dyp.at[c, chips + m], r_dyp.at[c, source], (me_d, partner))

    def first(c):
        for source in [partner] + relayed:
            arrived(dy.at[0, own_rows(source), columns(c)], r_dyp.at[c, source])
        part = dot_nn(seen_rows(0), dy[0, :, columns(c)]).reshape(n_dp, block, wide)
        total[c] = part + (total[c] if c < early else from_query(c))
        for at in range(line):
            pair_out[c, at] = total[c, at * inner + 1 - y].astype(jnp.bfloat16)
        send(pair_out.at[c], pair_in.at[c], s_p.at[c], r_p.at[c], (across, me_g))

    def second(c):
        arrived(pair_in.at[c], r_p.at[c])
        summed = lambda at: total[c, at * inner + y] + pair_in[c, at].astype(jnp.float32)
        for j in range(1, line):
            line_out[c, j] = summed(z_at(j)).astype(jnp.bfloat16)
            send(
                line_out.at[c, j], line_in.at[c, j], s_l.at[c, j], r_l.at[c, j],
                (z_at(j) * inner + y, me_g),
            )
        kept[c] = summed(z)

    def third(c):
        value = kept[c]
        for j in range(1, line):
            arrived(line_in.at[c, j], r_l.at[c, j])
            value += line_in[c, j].astype(jnp.float32)
        out[:, columns(c)] = value

    lag = 3
    for source in others:
        arrived(turned.at[0, :, :, own_rows(source)], r_feat.at[0, source])
    pass_on(0)
    for c in range(chunks):
        if c + 1 < chunks:
            pass_on(c + 1)
        first(c)
        if c >= lag:
            second(c - lag)
    for c in range(max(0, chunks - lag), chunks):
        second(c)
    for c in range(chunks):
        third(c)
    for condition, copy in unsent:
        if condition is None:
            copy.wait_send()
        else:
            pl.when(condition)(copy.wait_send)


def chip_step(pass_feats, query_feats, head, ids, n_dp, n_group, block):
    rows, width = pass_feats.shape
    emb = head.shape[1]
    line, chips = n_dp // 2, n_group // 2
    chunks = emb // 128
    slabs = max(1, emb // 256)
    wide = emb // chunks
    bf16 = lambda *shape: pltpu.VMEM(shape, jnp.bfloat16)
    f32 = lambda *shape: pltpu.VMEM(shape, jnp.float32)
    i32 = lambda *shape: pltpu.VMEM(shape, jnp.int32)
    sems = lambda *shape: [pltpu.SemaphoreType.DMA(shape)]
    pairs = lambda *shape: sems(*shape) * 2
    anywhere = pl.BlockSpec(memory_space=pl.ANY)
    return pl.pallas_call(
        functools.partial(chip_kernel, n_dp, n_group, chunks, slabs),
        out_shape=(
            jax.ShapeDtypeStruct((block, emb), jnp.float32),
            jax.ShapeDtypeStruct((1, rows), jnp.float32),
        ),
        in_specs=[anywhere, anywhere, anywhere, VMEM],
        out_specs=(VMEM, VMEM),
        scratch_shapes=[
            bf16(2 * rows, width), bf16(width, emb), bf16(2, rows, emb),
            f32(2, emb), f32(n_dp, 2, emb), f32(2, emb), f32(n_group, 2, emb),
            i32(8, rows), i32(n_dp, 8, rows),
            f32(2, rows, emb), f32(2, rows, 1), bf16(2, n_group, rows, emb),
            bf16(n_dp, rows, emb), bf16(n_dp, rows, emb), bf16(n_dp, rows, emb),
            f32(n_group, rows, rows), f32(n_dp, rows, rows),
            bf16(n_group, rows, rows), bf16(n_group, rows, rows),
            f32(n_dp, 8, rows), f32(n_dp, 8, rows),
            bf16(2, n_dp, n_group, block, rows), bf16(2, n_dp, block, n_group * rows),
            bf16(2, n_group * rows, emb),
            f32(chunks, n_dp, block, wide),
            bf16(chunks, line, block, wide), bf16(chunks, line, block, wide),
            bf16(chunks, line, block, wide), bf16(chunks, line, block, wide),
            f32(chunks, block, wide),
        ]
        + sems(2) + sems(slabs) + sems(2) + pairs(n_dp) + pairs(n_group) + pairs(n_dp)
        + sems(2, 2, line) + sems(2, line) + sems(2, n_dp) + pairs(2)
        + sems(2, 2 * chips) + sems(2, n_group)
        + sems(2, n_group) + sems(2, n_group)
        + pairs(n_group) + pairs(n_dp)
        + sems(2 * chips) + sems(n_group)
        + sems(chunks, 2 * chips) + sems(chunks, n_group)
        + pairs(chunks) + pairs(chunks, line),
        compiler_params=pltpu.CompilerParams(
            has_side_effects=True, collective_id=0, vmem_limit_bytes=60 * 2**20
        ),
        name="chip_step",
    )(pass_feats, query_feats, head, ids)


def body(query_feats, passage_feats, head, neg_ids):
    rows, width = query_feats.shape
    emb = head.shape[1]
    n_dp = lax.axis_size("dp")
    n_group = lax.axis_size("group")
    block = width // (n_dp * n_group)
    if n_dp <= 16 and n_dp % 2 == 0 and n_group % 2 == 0 and block % 128 == 0:
        head_grad, query_loss = chip_step(
            passage_feats, query_feats, head, neg_ids.T, n_dp, n_group, block
        )
        return (head_grad, query_loss.reshape(rows))

    def cut(feats):
        if block % 128 == 0:
            return feats
        feats = feats.reshape(rows, n_dp, n_group, block)
        return feats.transpose(2, 0, 1, 3).reshape(n_group, rows, n_dp * block)

    proj_query = jnp.dot(query_feats, head, preferred_element_type=jnp.float32).astype(jnp.bfloat16)
    proj_pass = jnp.dot(passage_feats, head, preferred_element_type=jnp.float32).astype(
        jnp.bfloat16
    )
    col_high = jnp.maximum(jnp.max(proj_query, axis=0), jnp.max(proj_pass, axis=0)).astype(
        jnp.float32
    )
    col_low = jnp.minimum(jnp.min(proj_query, axis=0), jnp.min(proj_pass, axis=0)).astype(
        jnp.float32
    )
    named = (neg_ids // (n_group * rows)) * rows + neg_ids % rows
    head_grad, query_loss = whole_step(
        proj_query, proj_pass, jnp.stack([col_high, -col_low]), cut(query_feats),
        cut(passage_feats), named, n_dp, n_group, block,
    )
    return (head_grad, query_loss.reshape(rows))


def solution(mesh):
    return jax.shard_map(
        body,
        mesh=mesh,
        in_specs=(
            P(("dp", "group"), None),
            P(("dp", "group"), None),
            P(),
            P(("dp", "group"), None),
        ),
        out_specs=(P(("dp", "group"), None), P(("dp", "group"))),
        check_vma=False,
    )
```

```python
import functools
import math

import jax
import jax.numpy as jnp
from jax import lax
from jax.experimental import pallas as pl
from jax.experimental.pallas import tpu as pltpu
from jax.sharding import PartitionSpec as P

scaling_divisor = 0.05
levels = 15.0
epsilon = 1e-06
MESH = pl.DeviceIdType.MESH
VMEM = pl.BlockSpec(memory_space=pltpu.VMEM)


def quantize(projected, low, stride, inv_stride):
    level = (projected.astype(jnp.float32) - low) * inv_stride
    turn = level - jnp.floor(level + 0.5)
    quarter = 0.25 - jnp.abs(jnp.abs(turn) - 0.25)
    angle = jnp.where(turn < 0, -quarter, quarter) * (2.0 * math.pi)
    square = angle * angle
    series = -1.0 / math.factorial(11)
    for order in (9, 7, 5, 3, 1):
        series = (-1.0) ** (order // 2) / math.factorial(order) + square * series
    return low + stride * (level - angle * series * (1.0 / (2.0 * math.pi)))


def norm_back(cotangent, quantized, inverse):
    inner_prod = jnp.sum(quantized * cotangent, axis=-1, keepdims=True)
    return (inverse * cotangent - quantized * (inverse**3 * inner_prod)).astype(jnp.bfloat16)


def dot_nn(a, b):
    return jnp.dot(a, b, preferred_element_type=jnp.float32)


def dot_nt(a, b):
    return lax.dot_general(a, b, (((1,), (1,)), ((), ())), preferred_element_type=jnp.float32)


def dot_tn(a, b):
    return lax.dot_general(a, b, (((0,), (0,)), ((), ())), preferred_element_type=jnp.float32)


def remote(src, dst, send, recv, device):
    return pltpu.make_async_remote_copy(
        src_ref=src,
        dst_ref=dst,
        send_sem=send,
        recv_sem=recv,
        device_id=device,
        device_id_type=MESH,
    )


def step_kernel(
    n_dp, n_group, inner, chunks,
    proj_query, proj_pass, stats, query_feats, pass_feats, named, out, loss,
    stats_group, stats_dp, stats_mid,
    emb_query, emb_pass, quant_query, quant_pass, inv_query, inv_pass,
    batch_query, batch_pass, dp_query, dp_pass, hard_exp,
    batch_out, batch_in, hard_out, hard_in,
    feats, turned, dy, gathered, total, pair_out, pair_in, line_out, line_in, kept,
    s_stat_g, r_stat_g, s_stat_d, r_stat_d, s_feat, r_feat,
    s_line, s_pair, r_dp, s_batch, r_batch, s_bw, r_bw, s_hw, r_hw,
    s_dy, r_dy, s_p, r_p, s_l, r_l, *staged
):
    me_d, me_g = lax.axis_index("dp"), lax.axis_index("group")
    line = n_dp // inner
    z, y = me_d // inner, lax.rem(me_d, inner)
    rows, emb = proj_query.shape
    wide = emb // chunks
    block = out.shape[0]
    columns = lambda c: pl.ds(c * wide, wide)
    group_at = lambda k: lax.rem(me_g + k, n_group)
    group_from = lambda k: lax.rem(me_g + n_group - k, n_group)
    dp_at = lambda k: lax.rem(me_d + k, n_dp)
    dp_from = lambda k: lax.rem(me_d + n_dp - k, n_dp)

    cut_feats = (staged[0].at[0], staged[0].at[1]) if staged else (query_feats, pass_feats)

    def feat_copy(i, k):
        src = cut_feats[i]
        return remote(
            src.at[group_at(k)], feats.at[i, k], s_feat.at[i, k], r_feat.at[i, k], (me_d, group_at(k))
        )

    def largest(src, landing, send, recv, count, target):
        copies = []
        for k in range(1, count):
            copies.append(remote(src, landing.at[k], send.at[k], recv.at[k], target(k)))
            copies[-1].start()
        value = src[...]
        for k in range(1, count):
            copies[k - 1].wait()
            value = jnp.maximum(value, landing[k])
        return value

    if staged:
        for i, whole in enumerate((query_feats, pass_feats)):
            for d in range(n_dp):
                for g in range(n_group):
                    staged[0][i, g, :, d * block : (d + 1) * block] = whole[
                        :, (d * n_group + g) * block : (d * n_group + g + 1) * block
                    ]

    stats_mid[...] = largest(
        stats, stats_group, s_stat_g, r_stat_g, n_group, lambda k: (me_d, group_at(k))
    )
    for i in range(2):
        for k in range(1, n_group):
            feat_copy(i, k).start()
    bounds = largest(stats_mid, stats_dp, s_stat_d, r_stat_d, n_dp, lambda k: (dp_at(k), me_g))
    high, low = bounds[0:1], -bounds[1:2]
    stride = (high - low) / levels
    inv_stride = 1.0 / stride

    items = ((emb_pass, batch_pass, dp_pass), (emb_query, batch_query, dp_query))

    def slot_copy(i, source, src, send, target):
        return remote(src, items[i][2].at[source], send, r_dp.at[i, source], (target, me_g))

    def forwards(i, at, src, rightward, leftward):
        source = at * inner + y
        copies = []
        if rightward:
            copies.append((z < line - 1, slot_copy(i, source, src, s_line.at[i, 0, at], dp_at(inner))))
        if leftward:
            copies.append((z > 0, slot_copy(i, source, src, s_line.at[i, 1, at], dp_from(inner))))
        for k in range(1, inner):
            target = z * inner + lax.rem(y + k, inner)
            copies.append((None, slot_copy(i, source, src, s_pair.at[i, k, at], target)))
        return copies

    def each(copies, act):
        for condition, copy in copies:
            if condition is None:
                act(copy)
            else:
                pl.when(condition)(functools.partial(act, copy))

    def start(copy):
        copy.start()

    def wait_send(copy):
        copy.wait_send()

    def batch_copy(i, k):
        return remote(
            items[i][0], items[i][1].at[k], s_batch.at[i, k], r_batch.at[i, k], (me_d, group_at(k))
        )

    def start_own(i):
        each(forwards(i, z, items[i][0], True, True), start)
        for k in range(1, n_group):
            batch_copy(i, k).start()

    def relay(i, s):
        for at, inside, onward in ((z - s, z >= s, True), (z + s, z + s < line, False)):

            @pl.when(inside)
            def _(at=at, onward=onward):
                source = at * inner + y
                arrived = items[i][2].at[source]
                slot_copy(i, source, arrived, s_line.at[i, 0, at], me_d).wait_recv()
                each(forwards(i, at, arrived, onward, not onward), start)

    def wait_pairs(i):
        for k in range(1, inner):
            for at in range(line):
                source = at * inner + lax.rem(y + k, inner)
                arrived = items[i][2].at[source]
                slot_copy(i, source, arrived, s_pair.at[i, k, at], me_d).wait_recv()

    def wait_all_sent(i):
        each(forwards(i, z, items[i][0], True, True), wait_send)
        for s in range(1, line):
            for at, inside, onward in ((z - s, z >= s, True), (z + s, z + s < line, False)):

                @pl.when(inside)
                def _(at=at, onward=onward):
                    arrived = items[i][2].at[at * inner + y]
                    each(forwards(i, at, arrived, onward, not onward), wait_send)

    def embed(projected, quant, inverse, emb_ref):
        value = quantize(projected[...], low, stride, inv_stride)
        inv = lax.rsqrt(jnp.sum(value * value, axis=-1, keepdims=True) + epsilon)
        quant[...] = value
        inverse[...] = inv
        emb_ref[...] = (value * inv).astype(jnp.bfloat16)

    embed(proj_pass, quant_pass, inv_pass, emb_pass)
    start_own(0)
    embed(proj_query, quant_query, inv_query, emb_query)
    for s in range(1, line):
        relay(0, s)
    start_own(1)

    for i in range(2):
        for k in range(1, n_group):
            feat_copy(i, k).wait()
        lanes = pl.ds(i * rows, rows)
        turned[0, :, lanes] = cut_feats[i][me_g].T
        for k in range(1, n_group):
            turned[k, :, lanes] = feats[i, k].T

    for k in range(1, n_group):
        batch_copy(0, k).wait()
    wait_pairs(0)
    if line > 1:
        relay(1, 1)

    def over_dp(step, value):
        if n_dp > 16:
            return lax.fori_loop(1, n_dp, step, value)
        for k in range(1, n_dp):
            value = step(k, value)
        return value

    query = emb_query[...]
    eye = (
        lax.broadcasted_iota(jnp.int32, (rows, rows), 0)
        == lax.broadcasted_iota(jnp.int32, (rows, rows), 1)
    ).astype(jnp.float32)
    place = lax.broadcasted_iota(jnp.int32, (rows, rows), 1)
    batch_block = lambda k: emb_pass[...] if k == 0 else batch_pass[k]
    scores = [dot_nt(query, batch_block(k)) / scaling_divisor for k in range(n_group)]
    positive = jnp.sum(scores[0] * eye, axis=1, keepdims=True)
    exp_batch = [jnp.exp(score) for score in scores]
    batch_total = sum(jnp.sum(value, axis=1, keepdims=True) for value in exp_batch)
    exp_pos = jnp.exp(positive)

    def hard_step(k, hard_sum):
        source = dp_at(k)
        score = dot_nt(query, dp_pass[source]) / scaling_divisor
        here = named[:, 0:1] == place + source * rows
        for n in range(1, named.shape[1]):
            here = here | (named[:, n : n + 1] == place + source * rows)
        value = jnp.where(here, jnp.exp(score), 0.0)
        hard_exp[k] = value
        return hard_sum + value

    hard_sum = over_dp(hard_step, jnp.zeros((rows, rows), jnp.float32))
    hard_total = exp_pos + jnp.sum(hard_sum, axis=1, keepdims=True)
    column = jnp.log(batch_total) - positive + jnp.log(hard_total) - positive
    loss[...] = jnp.sum(column * eye, axis=0, keepdims=True)

    def weight_copy(k):
        return remote(
            batch_out.at[k], batch_in.at[k], s_bw.at[k], r_bw.at[k], (me_d, group_from(k))
        )

    def hard_copy(k):
        return remote(hard_out.at[k], hard_in.at[k], s_hw.at[k], r_hw.at[k], (dp_at(k), me_g))

    for k in range(n_group):
        weight = exp_batch[k] / batch_total
        if k == 0:
            weight = weight - eye * (2.0 - exp_pos / hard_total)
        batch_out[k] = weight.astype(jnp.bfloat16)
        if k:
            weight_copy(k).start()

    def hard_send(k, nothing):
        hard_out[k] = (hard_exp[k] / hard_total).astype(jnp.bfloat16)
        hard_copy(k).start()
        return nothing

    over_dp(hard_send, 0)
    if line > 2:
        relay(1, 2)

    grad = dot_nn(batch_out[0], emb_pass[...])
    for k in range(1, n_group):
        grad += dot_nn(batch_out[k], batch_pass[k])
    grad = over_dp(lambda k, value: value + dot_nn(hard_out[k], dp_pass[dp_at(k)]), grad)
    dy[0] = norm_back(grad / scaling_divisor, quant_query[...], inv_query[...])

    def dy_copy(i, c, k):
        return remote(
            dy.at[i, :, columns(c)], gathered.at[k, pl.ds(i * rows, rows), columns(c)],
            s_dy.at[i, c, k], r_dy.at[i, c, k], (me_d, group_at(k)),
        )

    for c in range(chunks):
        for k in range(1, n_group):
            dy_copy(0, c, k).start()
    for s in range(3, line):
        relay(1, s)

    for k in range(1, n_group):
        batch_copy(1, k).wait()
        weight_copy(k).wait()
    grad = dot_tn(batch_out[0], emb_query[...])
    for k in range(1, n_group):
        grad += dot_tn(batch_in[k], batch_query[n_group - k])
    grad = grad / scaling_divisor
    wait_pairs(1)

    def hard_back(k, value):
        hard_copy(k).wait()
        weight = hard_in[k]
        one = jnp.sum(weight.astype(jnp.float32), axis=1, keepdims=True)
        hard = (one * dp_query[dp_from(k)].astype(jnp.float32) * (1.0 / scaling_divisor)).astype(
            jnp.bfloat16
        )
        chosen = jnp.where(weight.astype(jnp.float32) != 0, 1.0, 0.0).astype(jnp.bfloat16)
        return value + dot_tn(chosen, hard)

    dy[1] = norm_back(over_dp(hard_back, grad), quant_pass[...], inv_pass[...])
    for c in range(chunks):
        for k in range(1, n_group):
            dy_copy(1, c, k).start()

    def pair_copy(c, k):
        target = z * inner + lax.rem(y + k, inner)
        return remote(
            pair_out.at[c, k - 1], pair_in.at[c, k - 1], s_p.at[c, k], r_p.at[c, k], (target, me_g)
        )

    def line_copy(c, j):
        target = lax.rem(z + j, line) * inner + y
        return remote(
            line_out.at[c, j], line_in.at[c, j], s_l.at[c, j], r_l.at[c, j], (target, me_g)
        )

    def first(c):
        part = dot_nn(turned[0, :, 0:rows], dy[0, :, columns(c)])
        part += dot_nn(turned[0, :, rows:], dy[1, :, columns(c)])
        for k in range(1, n_group):
            dy_copy(0, c, k).wait()
            dy_copy(1, c, k).wait()
            part += dot_nn(turned[k], gathered[k, :, columns(c)])
        total[c] = part.reshape(n_dp, block, wide)
        for k in range(1, inner):
            for at in range(line):
                pair_out[c, k - 1, at] = total[c, at * inner + lax.rem(y + k, inner)].astype(
                    jnp.bfloat16
                )
            pair_copy(c, k).start()

    def second(c):
        for k in range(1, inner):
            pair_copy(c, k).wait()

        def summed(at):
            value = total[c, at * inner + y]
            for k in range(1, inner):
                value += pair_in[c, k - 1, at].astype(jnp.float32)
            return value

        for j in range(1, line):
            line_out[c, j] = summed(lax.rem(z + j, line)).astype(jnp.bfloat16)
            line_copy(c, j).start()
        kept[c] = summed(z)

    def third(c):
        value = kept[c]
        for j in range(1, line):
            line_copy(c, j).wait()
            value += line_in[c, j].astype(jnp.float32)
        out[:, columns(c)] = value

    for c in range(chunks):
        first(c)
        if c:
            second(c - 1)
    second(chunks - 1)
    for i in range(2):
        wait_all_sent(i)
    for c in range(chunks):
        third(c)


def whole_step(proj_query, proj_pass, stats, query_feats, pass_feats, named, n_dp, n_group, block):
    inner = 2 if n_dp % 2 == 0 else 1
    line = n_dp // inner
    rows, emb = proj_query.shape
    depth = n_dp * block
    inside = query_feats.ndim == 2
    chunks = max(1, emb // 256)
    wide = emb // chunks
    bf16 = lambda *shape: pltpu.VMEM(shape, jnp.bfloat16)
    f32 = lambda *shape: pltpu.VMEM(shape, jnp.float32)
    sems = lambda *shape: [pltpu.SemaphoreType.DMA(shape)]
    pairs = lambda *shape: sems(*shape) * 2
    return pl.pallas_call(
        functools.partial(step_kernel, n_dp, n_group, inner, chunks),
        out_shape=(
            jax.ShapeDtypeStruct((block, emb), jnp.float32),
            jax.ShapeDtypeStruct((1, rows), jnp.float32),
        ),
        in_specs=[VMEM] * 6,
        out_specs=(VMEM, VMEM),
        scratch_shapes=[
            f32(n_group, 2, emb), f32(n_dp, 2, emb), f32(2, emb),
            bf16(rows, emb), bf16(rows, emb), f32(rows, emb), f32(rows, emb), f32(rows, 1), f32(rows, 1),
            bf16(n_group, rows, emb), bf16(n_group, rows, emb), bf16(n_dp, rows, emb), bf16(n_dp, rows, emb),
            f32(n_dp, rows, rows),
            bf16(n_group, rows, rows), bf16(n_group, rows, rows), bf16(n_dp, rows, rows), bf16(n_dp, rows, rows),
            bf16(2, n_group, rows, depth), bf16(n_group, depth, 2 * rows), bf16(2, rows, emb),
            bf16(n_group, 2 * rows, emb),
            f32(chunks, n_dp, block, wide),
            bf16(chunks, max(1, inner - 1), line, block, wide),
            bf16(chunks, max(1, inner - 1), line, block, wide),
            bf16(chunks, line, block, wide), bf16(chunks, line, block, wide),
            f32(chunks, block, wide),
        ]
        + pairs(n_group) + pairs(n_dp) + pairs(2, n_group)
        + sems(2, 2, line) + sems(2, inner, line) + sems(2, n_dp) + pairs(2, n_group)
        + pairs(n_group) + pairs(n_dp)
        + pairs(2, chunks, n_group) + pairs(chunks, inner) + pairs(chunks, line)
        + ([bf16(2, n_group, rows, depth)] if inside else []),
        compiler_params=pltpu.CompilerParams(has_side_effects=True, vmem_limit_bytes=67043328),
        name="step",
    )(proj_query, proj_pass, stats, query_feats, pass_feats, named)


def chip_kernel(
    n_dp, n_group, chunks, slabs,
    pass_hbm, query_hbm, head_hbm, ids,
    out, loss,
    lhs, head, acc, proj, stats, stats_dp, stats_mid, stats_group, ids_own, ids_in,
    quant, inv, batch, dp_pass, dp_query, emb_dp,
    exp_batch, hard_exp, batch_out, batch_in, row_out, row_in,
    sent_feats, turned, dy, total, pair_out, pair_in, line_out, line_in, kept,
    l_feat, l_head, l_own, l_out, s_stat_d, r_stat_d, s_stat_g, r_stat_g, s_ids, r_ids,
    s_line, s_pair, r_dp, s_half, r_half, s_batch, r_batch, s_feat, r_feat, s_bw, r_bw, s_row, r_row,
    s_dyq, r_dyq, s_dyp, r_dyp, s_p, r_p, s_l, r_l,
):
    me_d, me_g = lax.axis_index("dp"), lax.axis_index("group")
    inner = 2
    line = n_dp // inner
    z, y = me_d // inner, lax.rem(me_d, inner)
    chips = n_group // 2
    chip, core = me_g // 2, lax.rem(me_g, 2)
    rows, emb = proj.shape[1:]
    wide = emb // chunks
    slab = head.shape[0] // slabs
    block = out.shape[0]
    columns = lambda c: pl.ds(c * wide, wide)
    own_rows = lambda g: pl.ds(pl.multiple_of(g * rows, rows), rows)
    group_at = lambda k: lax.rem(me_g + k, n_group)
    dp_at = lambda k: lax.rem(me_d + k, n_dp)
    dp_from = lambda k: lax.rem(me_d + n_dp - k, n_dp)
    z_at = lambda k: lax.rem(z + k, line)

    def plane(k):
        value = z
        for bit in range(k.bit_length()):
            if k >> bit & 1:
                value = value + (1 - 2 * lax.rem(z // (1 << bit), 2)) * (1 << bit)
        return value

    half = rows // 2
    partner = chip * 2 + 1 - core
    beside = [lax.rem(chip + j, chips) * 2 + core for j in range(1, chips)]
    relayed = [lax.rem(chip + j, chips) * 2 + 1 - core for j in range(1, chips)]
    others = [partner] + beside + relayed
    across = z * inner + 1 - y

    unsent = []

    def send(src, dst, send_sem, recv_sem, device, condition=None):
        copy = remote(src, dst, send_sem, recv_sem, device)
        if condition is None:
            copy.start()
        else:
            pl.when(condition)(copy.start)
        unsent.append((condition, copy))

    def arrived(dst, recv_sem):
        remote(dst, dst, recv_sem, recv_sem, (me_d, partner)).wait_recv()

    barrier = pltpu.get_barrier_semaphore()
    peers = [(me_d, group_at(k)) for k in range(1, n_group)] + [(dp_at(k), me_g) for k in range(1, n_dp)]
    for peer in peers:
        pl.semaphore_signal(barrier, inc=1, device_id=peer, device_id_type=MESH)

    loads = []
    for s in range(slabs):
        piece = pl.ds(s * slab, slab)
        for i, source in enumerate((pass_hbm, query_hbm)):
            loads.append(
                pltpu.make_async_copy(
                    source.at[:, piece], lhs.at[pl.ds(i * rows, rows), piece], l_feat.at[i, s]
                )
            )
        loads.append(pltpu.make_async_copy(head_hbm.at[piece], head.at[piece], l_head.at[s]))
    for copy in loads:
        copy.start()
    ids_own[...] = jnp.full(ids_own.shape, -1, jnp.int32)
    ids_own[0 : ids.shape[0]] = ids[...]
    for s in range(slabs):
        for copy in loads[3 * s : 3 * s + 3]:
            copy.wait()
        piece = slice(s * slab, (s + 1) * slab)
        part = dot_nn(lhs[:, piece], head[piece])
        if s:
            part = acc[...] + part
        if s < slabs - 1:
            acc[...] = part
        for d in range(s * slab // block, (s + 1) * slab // block):
            for i in range(2):
                sent_feats[i, d // n_group, d % n_group] = lhs[
                    i * rows : (i + 1) * rows, d * block : (d + 1) * block
                ].T
    rounded = part.astype(jnp.bfloat16)
    proj[0] = rounded[:rows]
    proj[1] = rounded[rows:]
    seen = rounded.astype(jnp.float32)
    stats[0:1] = jnp.max(seen, axis=0, keepdims=True)
    stats[1:2] = -jnp.min(seen, axis=0, keepdims=True)
    pl.semaphore_wait(barrier, len(peers))

    for k in range(1, n_dp):
        send(stats, stats_dp.at[k], s_stat_d.at[k], r_stat_d.at[k], (dp_at(k), me_g))

    dp_bufs = (dp_pass, dp_query)

    def along(i, at, src, rightward, leftward):
        source = at * inner + y
        dst = dp_bufs[i].at[source]
        if rightward:
            send(src, dst, s_line.at[i, 0, at], r_dp.at[i, source], (dp_at(inner), me_g), z < line - 1)
        if leftward:
            send(src, dst, s_line.at[i, 1, at], r_dp.at[i, source], (dp_from(inner), me_g), z > 0)

    def over(i, at, src):
        source = at * inner + y
        send(src, dp_bufs[i].at[source], s_pair.at[i, at], r_dp.at[i, source], (across, me_g))

    def relay(i, s):
        for at, inside, onward in ((z - s, z >= s, 0), (z + s, z + s < line, 1)):
            source = at * inner + y
            landed = dp_bufs[i].at[source]
            part = landed.at[pl.ds(0, half)]
            if onward == 0:
                target, more, twin = dp_at(inner), inside & (z < line - 1), lax.rem(z, 2) == 1
            else:
                target, more, twin = dp_from(inner), inside & (z > 0), lax.rem(z, 2) == 0
            recv = r_dp.at[i, source]
            steps = [(more, remote(landed, landed, s_line.at[i, onward, at], recv, (target, me_g)))]
            side = remote(landed, landed, s_pair.at[i, at], recv, (across, me_g))
            if s == 1:
                steps.append((inside & jnp.logical_not(twin), side))
                steps.append(
                    (inside & twin, remote(part, part, s_pair.at[i, at], recv, (across, me_g)))
                )
            else:
                steps.append((inside, side))

            @pl.when(inside)
            def _(landed=landed, recv=recv):
                arrived(landed, recv)

            for condition, copy in steps:
                pl.when(condition)(copy.start)
                unsent.append((condition, copy))

    def lower(i):
        arrived(dp_bufs[i].at[across], r_dp.at[i, across])
        part = dp_bufs[i].at[across, pl.ds(half, half)]
        send(part, part, s_half.at[i], r_half.at[i], (plane(1) * inner + y, me_g))

    def gathered(i, k):
        source = plane(k) * inner + 1 - y
        landed = dp_bufs[i].at[source]
        if k == 1:
            arrived(landed.at[pl.ds(0, half)], r_dp.at[i, source])
            arrived(landed.at[pl.ds(half, half)], r_half.at[i])
        else:
            arrived(landed, r_dp.at[i, source])
        return source

    def send_feats(i, which):
        for m, target in enumerate(others):
            if m in which:
                send(
                    sent_feats.at[i, :, target], turned.at[i, :, :, own_rows(me_g)],
                    s_feat.at[i, m], r_feat.at[i, me_g], (me_d, target),
                )

    along(0, z, proj.at[0], True, True)
    over(0, z, proj.at[0])
    for k in range(1, n_dp):
        send(ids_own, ids_in.at[k], s_ids.at[k], r_ids.at[k], (dp_at(k), me_g))

    bounds = stats[...]
    for k in range(1, n_dp):
        arrived(stats_dp.at[k], r_stat_d.at[k])
        bounds = jnp.maximum(bounds, stats_dp[k])
    stats_mid[...] = bounds
    for k in range(1, n_group):
        send(stats_mid, stats_group.at[k], s_stat_g.at[k], r_stat_g.at[k], (me_d, group_at(k)))
    send_feats(1, range(chips))
    relay(0, 1)
    for k in range(1, n_group):
        arrived(stats_group.at[k], r_stat_g.at[k])
        bounds = jnp.maximum(bounds, stats_group[k])
    high, low = bounds[0:1], -bounds[1:2]
    stride = (high - low) / levels
    inv_stride = 1.0 / stride

    def embed(projected):
        value = quantize(projected, low, stride, inv_stride)
        inverse = lax.rsqrt(jnp.sum(value * value, axis=-1, keepdims=True) + epsilon)
        return value, inverse, (value * inverse).astype(jnp.bfloat16)

    for i in range(2):
        quant[i], inv[i], batch[i, me_g] = embed(proj[i])
        own = batch.at[i, me_g]
        for m, target in enumerate([partner] + beside):
            send(own, own, s_batch.at[i, m], r_batch.at[i, me_g], (me_d, target))

    def hand_over(i):
        for m, source in enumerate(beside):
            landed = batch.at[i, source]
            arrived(landed, r_batch.at[i, source])
            send(landed, landed, s_batch.at[i, chips + m], r_batch.at[i, source], (me_d, partner))

    over(1, z, batch.at[1, me_g])
    send_feats(1, range(chips, n_group))
    stay = [
        pltpu.make_async_copy(
            sent_feats.at[i, :, me_g], turned.at[i, :, :, own_rows(me_g)], l_own.at[i]
        )
        for i in range(2)
    ]
    for copy in stay:
        copy.start()

    query = batch[1, me_g]
    eye = (
        lax.broadcasted_iota(jnp.int32, (rows, rows), 0)
        == lax.broadcasted_iota(jnp.int32, (rows, rows), 1)
    ).astype(jnp.float32)
    place = lax.broadcasted_iota(jnp.int32, (rows, rows), 0)

    def named(rows_of, device):
        base = (device * n_group + me_g) * rows
        here = rows_of[0:1] == place + base
        for n in range(1, ids.shape[0]):
            here = here | (rows_of[n : n + 1] == place + base)
        return here

    def hard_scores(source):
        _, _, block_emb = embed(dp_pass[source])
        emb_dp[source] = block_emb
        score = dot_nt(block_emb, query) / scaling_divisor
        hard_exp[source] = jnp.where(named(ids_own[...], source), jnp.exp(score), 0.0)

    if line > 2:
        relay(0, 2)
    lower(0)
    along(1, z, batch.at[1, me_g], True, True)
    hard_scores(across)
    hand_over(0)
    send_feats(0, range(chips))
    for s in range(3, line):
        relay(0, s)
    hand_over(1)

    for source in [partner] + relayed:
        arrived(batch.at[0, source], r_batch.at[0, source])
    own_score = dot_nt(batch[0, me_g], query) / scaling_divisor
    positive = jnp.sum(own_score * eye, axis=0, keepdims=True)
    own_exp = jnp.exp(own_score)
    batch_total = jnp.sum(own_exp, axis=0, keepdims=True)
    for m, source in enumerate(others):
        weight = jnp.exp(dot_nt(batch[0, source], query) / scaling_divisor)
        exp_batch[m] = weight
        batch_total += jnp.sum(weight, axis=0, keepdims=True)
    exp_pos = jnp.exp(positive)

    for k in range(1, line):
        hard_scores(plane(k) * inner + y)
    relay(1, 1)
    for k in range(1, line):
        hard_scores(gathered(0, k))

    hard_sum = hard_exp[dp_at(1)]
    for k in range(2, n_dp):
        hard_sum += hard_exp[dp_at(k)]
    hard_total = exp_pos + jnp.sum(hard_sum, axis=0, keepdims=True)
    loss[...] = jnp.log(batch_total) - positive + jnp.log(hard_total) - positive

    for m, target in enumerate(others):
        batch_out[target] = (exp_batch[m] / batch_total).astype(jnp.bfloat16)
        send(batch_out.at[target], batch_in.at[me_g], s_bw.at[m], r_bw.at[me_g], (me_d, target))
    own_weight = (own_exp / batch_total - eye * (2.0 - exp_pos / hard_total)).astype(jnp.bfloat16)
    grad = dot_tn(own_weight, batch[0, me_g])
    for source in others:
        grad += dot_tn(batch_out[source], batch[0, source])
    for k in range(1, n_dp):
        source = dp_at(k)
        weight = (hard_exp[source] / hard_total).astype(jnp.bfloat16)
        row = jnp.sum(weight.astype(jnp.float32), axis=0, keepdims=True)
        row_out[k] = jnp.broadcast_to(row, row_out.shape[1:])
        send(row_out.at[k], row_in.at[k], s_row.at[k], r_row.at[k], (source, me_g))
        grad += dot_tn(weight, emb_dp[source])
    dy[1, own_rows(me_g)] = norm_back(grad / scaling_divisor, quant[1], inv[1])
    own = dy.at[1, own_rows(me_g)]
    for m, target in enumerate([partner] + beside):
        send(own, own, s_dyq.at[m], r_dyq.at[me_g], (me_d, target))
    send_feats(0, range(chips, n_group))
    if line > 2:
        relay(1, 2)
    lower(1)
    for s in range(3, line):
        relay(1, s)

    for source in [partner] + relayed:
        arrived(batch.at[1, source], r_batch.at[1, source])
    grad = dot_nn(own_weight, query)
    for source in others:
        arrived(batch_in.at[source], r_bw.at[source])
        grad += dot_nn(batch_in[source], batch[1, source])
    grad = grad / scaling_divisor
    for k in range(1, n_dp):
        arrived(ids_in.at[k], r_ids.at[k])

    def hard_back(source):
        k = lax.rem(me_d + n_dp - source, n_dp)
        arrived(row_in.at[k], r_row.at[k])
        weight = jnp.sum(row_in[k][0:1] * eye, axis=1, keepdims=True)
        hard = (weight * dp_query[source].astype(jnp.float32) * (1.0 / scaling_divisor)).astype(
            jnp.bfloat16
        )
        chosen = jnp.where(named(ids_in[k], me_d), 1.0, 0.0).astype(jnp.bfloat16)
        return dot_nn(chosen, hard)

    grad += hard_back(across)
    for m, source in enumerate(beside):
        landed = dy.at[1, own_rows(source)]
        arrived(landed, r_dyq.at[source])
        send(landed, landed, s_dyq.at[chips + m], r_dyq.at[source], (me_d, partner))
    for k in range(1, line):
        grad += hard_back(plane(k) * inner + y)
    for copy in stay:
        copy.wait()
    for source in others:
        arrived(turned.at[1, :, :, own_rows(source)], r_feat.at[1, source])
    for source in [partner] + relayed:
        arrived(dy.at[1, own_rows(source)], r_dyq.at[source])
    depth = n_dp * block
    seen_rows = lambda i: turned[i].reshape(depth, n_group * rows)
    from_query = lambda c: dot_nn(seen_rows(1), dy[1, :, columns(c)]).reshape(n_dp, block, wide)
    early = min(2, chunks)
    for c in range(early):
        total[c] = from_query(c)
    for k in range(1, line):
        grad += hard_back(gathered(1, k))

    dy[0, own_rows(me_g)] = norm_back(grad, quant[0], inv[0])
    for c in range(chunks):
        own = dy.at[0, own_rows(me_g), columns(c)]
        for m, target in enumerate(beside):
            send(own, own, s_dyp.at[c, 1 + m], r_dyp.at[c, me_g], (me_d, target))
        send(own, own, s_dyp.at[c, 0], r_dyp.at[c, me_g], (me_d, partner))

    def pass_on(c):
        for m, source in enumerate(beside):
            landed = dy.at[0, own_rows(source), columns(c)]
            arrived(landed, r_dyp.at[c, source])
            send(landed, landed, s_dyp.at[c, chips + m], r_dyp.at[c, source], (me_d, partner))

    def first(c):
        for source in [partner] + relayed:
            arrived(dy.at[0, own_rows(source), columns(c)], r_dyp.at[c, source])
        part = dot_nn(seen_rows(0), dy[0, :, columns(c)]).reshape(n_dp, block, wide)
        total[c] = part + (total[c] if c < early else from_query(c))
        for j in [*range(1, line), 0]:
            pair_out[c, j] = total[c, z_at(j) * inner + 1 - y].astype(jnp.bfloat16)
            send(pair_out.at[c, j], pair_in.at[c, j], s_p.at[c, j], r_p.at[c, j], (across, me_g))

    def second(c):
        for j in [*range(1, line), 0]:
            arrived(pair_in.at[c, j], r_p.at[c, j])
            value = total[c, z_at(j) * inner + y] + pair_in[c, j].astype(jnp.float32)
            if j:
                line_out[c, j] = value.astype(jnp.bfloat16)
                send(
                    line_out.at[c, j], line_in.at[c, j], s_l.at[c, j], r_l.at[c, j],
                    (z_at(j) * inner + y, me_g),
                )
            else:
                kept[c] = value

    def leave(c):
        return pltpu.make_async_copy(kept.at[c], out.at[:, columns(c)], l_out.at[c])

    def third(c):
        value = kept[c]
        for j in range(1, line):
            arrived(line_in.at[c, j], r_l.at[c, j])
            value += line_in[c, j].astype(jnp.float32)
        kept[c] = value
        leave(c).start()

    lag = 3
    for source in others:
        arrived(turned.at[0, :, :, own_rows(source)], r_feat.at[0, source])
    pass_on(0)
    for c in range(chunks + lag + 2):
        if c + 1 < chunks:
            pass_on(c + 1)
        if c < chunks:
            first(c)
        if 0 <= c - lag < chunks:
            second(c - lag)
        if 0 <= c - lag - 2 < chunks:
            third(c - lag - 2)
    for c in range(chunks):
        leave(c).wait()
    for condition, copy in unsent:
        if condition is None:
            copy.wait_send()
        else:
            pl.when(condition)(copy.wait_send)


def chip_step(pass_feats, query_feats, head, ids, n_dp, n_group, block):
    rows, width = pass_feats.shape
    emb = head.shape[1]
    line, chips = n_dp // 2, n_group // 2
    chunks = emb // 128
    slabs = max(1, width // max(512, block))
    wide = emb // chunks
    bf16 = lambda *shape: pltpu.VMEM(shape, jnp.bfloat16)
    f32 = lambda *shape: pltpu.VMEM(shape, jnp.float32)
    i32 = lambda *shape: pltpu.VMEM(shape, jnp.int32)
    sems = lambda *shape: [pltpu.SemaphoreType.DMA(shape)]
    pairs = lambda *shape: sems(*shape) * 2
    anywhere = pl.BlockSpec(memory_space=pl.ANY)
    return pl.pallas_call(
        functools.partial(chip_kernel, n_dp, n_group, chunks, slabs),
        out_shape=(
            jax.ShapeDtypeStruct((block, emb), jnp.float32),
            jax.ShapeDtypeStruct((1, rows), jnp.float32),
        ),
        in_specs=[anywhere, anywhere, anywhere, VMEM],
        out_specs=(anywhere, VMEM),
        scratch_shapes=[
            bf16(2 * rows, width), bf16(width, emb), f32(2 * rows, emb), bf16(2, rows, emb),
            f32(2, emb), f32(n_dp, 2, emb), f32(2, emb), f32(n_group, 2, emb),
            i32(8, rows), i32(n_dp, 8, rows),
            f32(2, rows, emb), f32(2, rows, 1), bf16(2, n_group, rows, emb),
            bf16(n_dp, rows, emb), bf16(n_dp, rows, emb), bf16(n_dp, rows, emb),
            f32(n_group, rows, rows), f32(n_dp, rows, rows),
            bf16(n_group, rows, rows), bf16(n_group, rows, rows),
            f32(n_dp, 8, rows), f32(n_dp, 8, rows),
            bf16(2, n_dp, n_group, block, rows), bf16(2, n_dp, block, n_group * rows),
            bf16(2, n_group * rows, emb),
            f32(chunks, n_dp, block, wide),
            bf16(chunks, line, block, wide), bf16(chunks, line, block, wide),
            bf16(chunks, line, block, wide), bf16(chunks, line, block, wide),
            f32(chunks, block, wide),
        ]
        + sems(2, slabs) + sems(slabs) + sems(2) + sems(chunks) + pairs(n_dp) + pairs(n_group) + pairs(n_dp)
        + sems(2, 2, line) + sems(2, line) + sems(2, n_dp) + pairs(2)
        + sems(2, 2 * chips) + sems(2, n_group)
        + sems(2, n_group) + sems(2, n_group)
        + pairs(n_group) + pairs(n_dp)
        + sems(2 * chips) + sems(n_group)
        + sems(chunks, 2 * chips) + sems(chunks, n_group)
        + pairs(chunks, line) + pairs(chunks, line),
        compiler_params=pltpu.CompilerParams(
            has_side_effects=True, collective_id=0, vmem_limit_bytes=60 * 2**20
        ),
        name="chip_step",
    )(pass_feats, query_feats, head, ids)


def body(query_feats, passage_feats, head, neg_ids):
    rows, width = query_feats.shape
    emb = head.shape[1]
    n_dp = lax.axis_size("dp")
    n_group = lax.axis_size("group")
    block = width // (n_dp * n_group)
    if n_dp <= 16 and n_dp % 2 == 0 and n_group % 2 == 0 and block % 128 == 0:
        head_grad, query_loss = chip_step(
            passage_feats, query_feats, head, neg_ids.T, n_dp, n_group, block
        )
        return (head_grad, query_loss.reshape(rows))

    def cut(feats):
        if block % 128 == 0:
            return feats
        feats = feats.reshape(rows, n_dp, n_group, block)
        return feats.transpose(2, 0, 1, 3).reshape(n_group, rows, n_dp * block)

    proj_query = jnp.dot(query_feats, head, preferred_element_type=jnp.float32).astype(jnp.bfloat16)
    proj_pass = jnp.dot(passage_feats, head, preferred_element_type=jnp.float32).astype(
        jnp.bfloat16
    )
    col_high = jnp.maximum(jnp.max(proj_query, axis=0), jnp.max(proj_pass, axis=0)).astype(
        jnp.float32
    )
    col_low = jnp.minimum(jnp.min(proj_query, axis=0), jnp.min(proj_pass, axis=0)).astype(
        jnp.float32
    )
    named = (neg_ids // (n_group * rows)) * rows + neg_ids % rows
    head_grad, query_loss = whole_step(
        proj_query, proj_pass, jnp.stack([col_high, -col_low]), cut(query_feats),
        cut(passage_feats), named, n_dp, n_group, block,
    )
    return (head_grad, query_loss.reshape(rows))


def solution(mesh):
    return jax.shard_map(
        body,
        mesh=mesh,
        in_specs=(
            P(("dp", "group"), None),
            P(("dp", "group"), None),
            P(),
            P(("dp", "group"), None),
        ),
        out_specs=(P(("dp", "group"), None), P(("dp", "group"))),
        check_vma=False,
    )
```
